32 devices in a mesh: groups: 2 (over x), context: 16 (over z, y, core).
Axes of the slice: x: 2, y: 2, z: 4, core: 2. Of those that a mesh axis runs over, the one named last changes fastest.
Arguments:
- queries: bfloat16 [4096, 16, 128], P(('groups', 'context')), parts along dimension 0, may hold values from -24 to 24
- keys: bfloat16 [4096, 8, 128], P(('groups', 'context')), parts along dimension 0, may hold values from -24 to 24
- values: bfloat16 [4096, 8, 128], P(('groups', 'context')), parts along dimension 0, may hold values from -6 to 6
- grad_out: bfloat16 [4096, 16, 128], P(('groups', 'context')), parts along dimension 0, may hold values from -24 to 24
- readout: float32 [16, 128], replicated, may hold values from -4 to 4
- segments: int32 [4096], P(('groups', 'context')), parts along dimension 0, may hold values from 0 to 3, never falling along the last dimension, each value on 1 to 1024 neighbouring positions
- loss_mask: int32 [4096], P(('groups', 'context')), parts along dimension 0, may hold values from 0 to 1, as said below
- labels: int32 [4096], P(('groups', 'context')), parts along dimension 0, may hold values 0 or 1
Outputs:
- grad_queries: bfloat16 [4096, 16, 128], P(('groups', 'context')), parts along dimension 0
- grad_keys: bfloat16 [4096, 8, 128], P(('groups', 'context')), parts along dimension 0
- grad_values: bfloat16 [4096, 8, 128], P(('groups', 'context')), parts along dimension 0
The draws below stay inside these ranges and needn't reach their ends.
There are 2 independent parts, one for each index of `groups`. The reference program is written for one: setup_inputs(seed, part) draws one part's arguments, and reference() takes and returns one part's arrays. A program takes and returns all parts, laid end to end along the dimension named above; an argument that names none is the same for every part. Nothing has to cross between parts.
Inputs may be any that keep to these rules, and one draw needn't show every extreme that they name: `loss_mask`: every entry of the first 128 positions is 0.
All inputs are finite; a program needn't handle non-finite values. No bound on the sum of `labels` on one device may be relied on, other than what follows from the above.
Results may differ from the reference program's by a relative error of at most 0.025.
Values may be sent and summed in bfloat16 or wider, within the bound.
No kernel may reach another device: no remote copies, remote signals or barrier semaphores. Data moves between devices by JAX's collectives and lax.ppermute only.
A program may use at most 128 MiB of HBM per device.

```python
import math
import jax
import jax.numpy as jnp
import numpy as np
from jax import lax

HEADS = 16
KV_HEADS = 8
HEAD_DIM = 128
WINDOW = 1024
TOK_DEV = 128
TOKENS = 2048
DOCS = 4
DOC_MOST = 1024


def drawn_rows(key, salt, head_count):
    inner = jax.random.fold_in(key, salt)
    return jax.random.truncated_normal(inner, -4.0, 4.0, (TOKENS, head_count, HEAD_DIM), jnp.float32)


def draw_queries(key, part):
    base = drawn_rows(key, 1, HEADS)
    return base.astype(jnp.bfloat16)


def draw_keys(key, part):
    base = drawn_rows(key, 2, KV_HEADS)
    return base.astype(jnp.bfloat16)


def draw_loss_mask(key, part):
    first, second = jax.random.split(jax.random.fold_in(key, 5))
    block_count = TOKENS // TOK_DEV
    live_blocks = jax.random.randint(first, (block_count,), 0, 4) > 0
    live_blocks = jnp.where(jnp.arange(block_count) == 0, False, live_blocks)
    token_live = jax.random.randint(second, (TOKENS,), 0, 5) < 3
    return (jnp.repeat(live_blocks, TOK_DEV) & token_live).astype(jnp.int32)


def plant(values, own_key, smallest, high):
    dims = values.shape
    place = [jax.random.randint(jax.random.fold_in(own_key, axis), (), 0, dims[axis]) for axis in range(len(dims))]
    values = values.at[tuple(place)].set(smallest)
    longest = dims.index(max(dims))
    place[longest] = (place[longest] + 1) % dims[longest]
    return values.at[tuple(place)].set(high)


def level_of(rng, dims, cuts, least, high):
    def one(position, parts):
        steps = jax.random.uniform(jax.random.fold_in(jax.random.fold_in(rng, 6), position), (parts,), jnp.float32, least / len(cuts), high / len(cuts))
        return jnp.repeat(jnp.exp(steps), dims[position] // parts).reshape((-1,) + (1,) * (len(dims) - position - 1))

    gain = one(*cuts[0])
    for cut in cuts[1:]:
        gain = gain * one(*cut)
    return gain


def split_up(amount, total, limit, skew):
    loads = [(1 << 20) // math.isqrt(rank ** skew) + 1 for rank in range(2, amount + 1)]
    rest, given = total - limit - (amount - 1), [1] * (amount - 1)
    while rest > 0:
        candidates = [i for i in range(amount - 1) if given[i] < limit]
        mass, remaining = sum([loads[i] for i in candidates]), rest
        for i in candidates:
            extra = min(limit - given[i], max(1, remaining * loads[i] // mass), rest)
            given[i] = given[i] + extra
            rest = rest - extra
    return np.array([limit] + given)


def ragged_sizes(stream_key, amount, total, most, skew):
    if amount == 2:
        one = jax.random.randint(stream_key, (), max(1, total - most), min(most, total - 1) + 1)
        return jnp.stack([one, total - one])
    lengths = jnp.asarray(split_up(amount, total, most, skew), jnp.int32)
    pairs = (amount - 1) // 2
    donor, taker = lengths[1:1 + 2 * pairs:2], lengths[2:2 + 2 * pairs:2]
    slack = jnp.minimum(donor - 1, most - taker)
    passed = jax.random.randint(jax.random.fold_in(stream_key, 1), (pairs,), 0, 1 << 20) % (slack + 1)
    lengths = lengths.at[1:1 + 2 * pairs:2].set(donor - passed).at[2:2 + 2 * pairs:2].set(taker + passed)
    return lengths[jax.random.permutation(jax.random.fold_in(stream_key, 2), amount)]


def normal_values(stream_key, extent, scale, bound, cuts=(), kind=jnp.bfloat16):
    level = level_of(stream_key, extent, cuts, -0.22, 0.18) if cuts else 1.0
    drawn = jax.random.normal(stream_key, extent, jnp.float32) * scale * level
    return jnp.minimum(jnp.maximum(drawn, -bound), bound).astype(kind)


def setup_inputs(seed: int = 0, part: int = 0) -> dict:
    streams_of = jax.random.split(jax.random.key(seed), 9)
    part_keys = jax.random.split(jax.random.fold_in(streams_of[8], part), 9)
    return {
        "queries": draw_queries(jax.random.fold_in(jax.random.fold_in(streams_of[8], part), 71), part),
        "keys": draw_keys(jax.random.fold_in(jax.random.fold_in(streams_of[8], part), 71), part),
        "values": normal_values(part_keys[2], (TOKENS, KV_HEADS, HEAD_DIM), 1.0, 6.0, ((0, 16),)),
        "grad_out": normal_values(part_keys[3], (TOKENS, HEADS, HEAD_DIM), 4.0, 24.0, ((0, 16),)),
        "readout": normal_values(streams_of[4], (HEADS, HEAD_DIM), 1.0, 4.0, (), jnp.float32),
        "segments": jnp.searchsorted(jnp.cumsum(ragged_sizes(part_keys[5], DOCS, TOKENS, DOC_MOST, 1)), jnp.arange(TOKENS), side="right").astype(jnp.int32),
        "loss_mask": draw_loss_mask(jax.random.fold_in(jax.random.fold_in(streams_of[8], part), 71), part),
        "labels": plant((jax.random.randint(part_keys[7], (TOKENS,), 0, 2) < 1).astype(jnp.int32), jax.random.fold_in(part_keys[7], 1), 0, 1),
    }


SCALE = 168.0 ** -0.5
NEGATIVE = -1e30


def block_inputs(block_id, queries, key_pad, value_pad, segments, seg_pad):
    start = (block_id * TOK_DEV).astype(jnp.int32)
    query_part = lax.dynamic_slice_in_dim(queries, start, TOK_DEV, 0)
    key_part = lax.dynamic_slice_in_dim(key_pad, start, TOK_DEV + WINDOW, 0)
    value_part = lax.dynamic_slice_in_dim(value_pad, start, TOK_DEV + WINDOW, 0)
    seg_query = lax.dynamic_slice_in_dim(segments, start, TOK_DEV, 0)
    seg_key = lax.dynamic_slice_in_dim(seg_pad, start, TOK_DEV + WINDOW, 0)
    query_pos = start + jnp.arange(TOK_DEV, dtype=jnp.int32)
    key_pos = start - WINDOW + jnp.arange(TOK_DEV + WINDOW, dtype=jnp.int32)
    distance = query_pos[:, None] - key_pos[None, :]
    allowed = (distance >= 0) & (distance < WINDOW) & (key_pos[None, :] >= 0) & (seg_query[:, None] == seg_key[None, :])
    return start, query_part, key_part, value_part, allowed


def grouped(array):
    return array.reshape(array.shape[0], KV_HEADS, HEADS // KV_HEADS, HEAD_DIM).astype(jnp.float32)


def probabilities(query_part, key_part, allowed):
    scores = jnp.einsum("qgrd,kgd->grqk", grouped(query_part), key_part.astype(jnp.float32)) * SCALE
    mask = allowed[None, None]
    scores = jnp.where(mask, scores, NEGATIVE)
    row_max = jnp.max(scores, axis=-1, keepdims=True)
    row_total = jnp.sum(jnp.where(mask, jnp.exp(scores - row_max), 0.0), axis=-1, keepdims=True)
    log_total = row_max + jnp.log(row_total)
    return jnp.where(mask, jnp.exp(scores - log_total), 0.0)


def reference(queries, keys, values, grad_out, readout, segments, loss_mask, labels):
    blocks = TOKENS // TOK_DEV
    key_pad = jnp.concatenate([jnp.zeros((WINDOW, KV_HEADS, HEAD_DIM), keys.dtype), keys], axis=0)
    value_pad = jnp.concatenate([jnp.zeros((WINDOW, KV_HEADS, HEAD_DIM), values.dtype), values], axis=0)
    seg_pad = jnp.concatenate([jnp.full((WINDOW,), -1, jnp.int32), segments.astype(jnp.int32)], axis=0)
    block_ids = jnp.arange(blocks, dtype=jnp.int32)

    def forward(block_id):
        start, query_part, key_part, value_part, allowed = block_inputs(block_id, queries, key_pad, value_pad, segments, seg_pad)
        prob = probabilities(query_part, key_part, allowed)
        prob_low = prob.astype(jnp.bfloat16)
        out = jnp.einsum("grqk,kgd->qgrd", prob_low.astype(jnp.float32), value_part.astype(jnp.float32))
        return out.reshape(TOK_DEV, HEADS, HEAD_DIM)

    attn_out = lax.map(forward, block_ids).reshape(TOKENS, HEADS, HEAD_DIM)
    reward = jnp.sum(attn_out * readout[None], axis=(1, 2))
    live_rows = loss_mask.astype(jnp.float32)
    probe_grad = live_rows * (jax.nn.sigmoid(reward) - labels.astype(jnp.float32))
    grad_attn = (live_rows[:, None, None] * grad_out.astype(jnp.float32) + probe_grad[:, None, None] * readout[None]).astype(jnp.bfloat16)
    delta = jnp.sum(grad_attn.astype(jnp.float32) * attn_out, axis=-1)

    def backward(carry, block_id):
        key_acc, value_acc = carry
        start, query_part, key_part, value_part, allowed = block_inputs(block_id, queries, key_pad, value_pad, segments, seg_pad)
        prob = probabilities(query_part, key_part, allowed)
        prob_low = prob.astype(jnp.bfloat16)
        grad_part = grouped(lax.dynamic_slice_in_dim(grad_attn, start, TOK_DEV, 0))
        delta_part = lax.dynamic_slice_in_dim(delta, start, TOK_DEV, 0).reshape(TOK_DEV, KV_HEADS, HEADS // KV_HEADS)
        grad_prob = jnp.einsum("qgrd,kgd->grqk", grad_part, value_part.astype(jnp.float32))
        grad_score = (prob * (grad_prob - jnp.transpose(delta_part, (1, 2, 0))[..., None])).astype(jnp.bfloat16)
        query_grad = (jnp.einsum("grqk,kgd->qgrd", grad_score.astype(jnp.float32), key_part.astype(jnp.float32)) * SCALE).astype(jnp.bfloat16)
        key_term = jnp.einsum("grqk,qgrd->kgd", grad_score.astype(jnp.float32), grouped(query_part)) * SCALE
        value_term = jnp.einsum("grqk,qgrd->kgd", prob_low.astype(jnp.float32), grad_part)
        old_keys = lax.dynamic_slice_in_dim(key_acc, start, TOK_DEV + WINDOW, 0)
        old_values = lax.dynamic_slice_in_dim(value_acc, start, TOK_DEV + WINDOW, 0)
        zero = jnp.zeros((), jnp.int32)
        key_acc = lax.dynamic_update_slice(key_acc, old_keys + key_term, (start, zero, zero))
        value_acc = lax.dynamic_update_slice(value_acc, old_values + value_term, (start, zero, zero))
        return (key_acc, value_acc), query_grad.reshape(TOK_DEV, HEADS, HEAD_DIM)

    empty = jnp.zeros((TOKENS + WINDOW, KV_HEADS, HEAD_DIM), jnp.float32)
    (key_acc, value_acc), query_grads = lax.scan(backward, (empty, empty), block_ids)
    grad_queries = query_grads.reshape(TOKENS, HEADS, HEAD_DIM)
    grad_keys = key_acc[WINDOW:].astype(jnp.bfloat16)
    grad_values = value_acc[WINDOW:].astype(jnp.bfloat16)
    return (grad_queries, grad_keys, grad_values)
```

```python
import functools
import math

import jax
import jax.numpy as jnp
from jax import lax
from jax.experimental import pallas as pl
from jax.experimental.pallas import tpu as pltpu
from jax.sharding import PartitionSpec as P

WINDOW = 1024
SCALE = 168.0 ** (-0.5)
LOG2E = math.log2(math.e)
NEGATIVE = -1e30
BLOCK = 256
AUX = 8
NT = (((1,), (1,)), ((), ()))
NN = (((1,), (0,)), ((), ()))


def dot(a, b, dims):
    return lax.dot_general(a, b, dims, preferred_element_type=jnp.float32)


def forward_kernel(
    halo, index_ref, message_ref, own_ref, other_ref, seg_ref, readout_ref,
    prob_ref, out_ref, inverse_ref, reward_ref, low_ref,
    key_s, value_s, bound_s, score_s,
):
    heads, tokens = message_ref.shape[0], message_ref.shape[0] * 128
    key_blocks = own_ref.shape[0]
    shift = halo // BLOCK
    index = index_ref[0]
    head = lax.rem(index, heads)
    even = lax.rem(index, 2) == 0

    def place(keys, values):
        for s in range(key_blocks):
            key_s[s * 128 : (s + 1) * 128, :] = keys[s]
            value_s[:, s * 128 : (s + 1) * 128] = values[s].T

    @pl.when(even)
    def _():
        place(own_ref, other_ref)

    @pl.when(jnp.logical_not(even))
    def _():
        place(other_ref, own_ref)

    seg_all = seg_ref[...]
    seg = seg_all[key_blocks - heads :]
    row = lax.broadcasted_iota(jnp.int32, (heads, 128), 0)
    lane = lax.broadcasted_iota(jnp.int32, (heads, 128), 1)
    token = halo + row * 128 + lane
    low = token - (WINDOW - 1)
    begin = jnp.zeros((heads, 128), jnp.int32)
    for s in range(0, 4):
        count = jnp.sum(jnp.where(seg_all < s, 1, 0))
        begin = jnp.where(seg == s, count, begin)
    low = jnp.maximum(low, begin)
    bound_s[...] = low
    for i in range(tokens // BLOCK):
        low_ref[i] = lax.div(jnp.min(low[2 * i : 2 * i + 1]), BLOCK)

    weights = jnp.broadcast_to(readout_ref[pl.ds(head, 1), :], (128, 128)).T[:, :1]
    key_iota = lax.broadcasted_iota(jnp.int32, (BLOCK, BLOCK), 0)
    query_iota = lax.broadcasted_iota(jnp.int32, (BLOCK, BLOCK), 1)

    def query_block(i, _):
        query = message_ref[pl.ds(2 * i, 2), 0:128, :].reshape(BLOCK, 128)
        bound = jnp.concatenate(
            [bound_s[pl.ds(2 * i, 1), :], bound_s[pl.ds(2 * i + 1, 1), :]], axis=1
        )
        last = i + shift
        first = low_ref[i]

        def scores(kb):
            start = pl.multiple_of(kb * BLOCK, BLOCK)
            return dot(key_s[pl.ds(start, BLOCK), :], query, NT) * (SCALE * LOG2E)

        def tops(score):
            return jnp.max(score.reshape(BLOCK // 8, 8, BLOCK), axis=0)

        def score_step(kb, top):
            score = jnp.where(key_iota >= bound - kb * BLOCK, scores(kb), NEGATIVE)
            score_s[last - kb] = score
            return jnp.maximum(top, tops(score))

        score = jnp.where(
            (key_iota >= bound - last * BLOCK) & (key_iota <= query_iota), scores(last), NEGATIVE
        )
        score_s[0] = score
        top = lax.fori_loop(first, last, score_step, tops(score))
        top = jnp.max(top, axis=0, keepdims=True)

        def value_step(kb, carry):
            total, out = carry
            prob = jnp.exp2(score_s[last - kb] - top)
            total = total + jnp.sum(prob.reshape(BLOCK // 8, 8, BLOCK), axis=0)
            prob = prob.astype(jnp.bfloat16)
            prob_ref[i, last - kb] = prob
            start = pl.multiple_of(kb * BLOCK, BLOCK)
            return total, out + dot(value_s[:, pl.ds(start, BLOCK)], prob, NN)

        total, out = lax.fori_loop(
            first,
            last + 1,
            value_step,
            (jnp.zeros((8, BLOCK), jnp.float32), jnp.zeros((128, BLOCK), jnp.float32)),
        )
        inverse = 1.0 / jnp.sum(total, axis=0, keepdims=True)
        out = out * inverse
        out_ref[:, pl.ds(pl.multiple_of(i * BLOCK, BLOCK), BLOCK)] = out
        inverse_ref[pl.ds(i, 1), :] = inverse
        reward = jnp.sum(out * weights, axis=0, keepdims=True)
        reward_ref[pl.ds(2 * i, 1), :] = reward[:, :128]
        reward_ref[pl.ds(2 * i + 1, 1), :] = reward[:, 128:]
        return 0

    lax.fori_loop(0, tokens // BLOCK, query_block, 0)


def backward_kernel(
    halo, index_ref, low_ref, message_ref, own_ref, other_ref, grad_ref, readout_ref, reward_ref,
    flag_ref, prob_ref, out_ref, inverse_ref,
    query_ref, keep_ref, send_ref,
    key_s, value_s, grad_s, delta_s, query_s, key_grad_s, value_grad_s,
):
    heads, tokens = message_ref.shape[0], message_ref.shape[0] * 128
    key_blocks = own_ref.shape[0]
    shift = halo // BLOCK
    index = index_ref[0]
    head = lax.rem(index, heads)
    even = lax.rem(index, 2) == 0

    def place(keys, values):
        for s in range(key_blocks):
            key_s[:, s * 128 : (s + 1) * 128] = keys[s].T
            value_s[s * 128 : (s + 1) * 128, :] = values[s]

    @pl.when(even)
    def _():
        place(own_ref, other_ref)

    @pl.when(jnp.logical_not(even))
    def _():
        place(other_ref, own_ref)

    live = flag_ref[0]
    probe = live * (jax.nn.sigmoid(reward_ref[...]) - flag_ref[1])
    live_t, probe_t = live.T, probe.T
    weights = readout_ref[pl.ds(head, 1), :]
    for s in range(heads):
        grad = live_t[:, s : s + 1] * grad_ref[s].astype(jnp.float32)
        grad = (grad + probe_t[:, s : s + 1] * weights).astype(jnp.bfloat16)
        grad_s[s] = grad
        out = out_ref[:, s * 128 : (s + 1) * 128]
        delta_s[s // 2 : s // 2 + 1, (s % 2) * 128 : (s % 2 + 1) * 128] = jnp.sum(
            grad.astype(jnp.float32).T * out, axis=0, keepdims=True
        )

    key_grad_s[...] = jnp.zeros_like(key_grad_s)
    value_grad_s[...] = jnp.zeros_like(value_grad_s)

    def query_block(i, _):
        query = message_ref[pl.ds(2 * i, 2), 0:128, :].reshape(BLOCK, 128)
        grad = grad_s[pl.ds(2 * i, 2)].reshape(BLOCK, 128)
        inverse = inverse_ref[pl.ds(i, 1), :]
        delta = delta_s[pl.ds(i, 1), :]
        last = i + shift

        def step(kb, query_grad):
            rows = pl.ds(pl.multiple_of(kb * BLOCK, BLOCK), BLOCK)
            prob = prob_ref[i, last - kb].astype(jnp.float32) * inverse
            value_grad_s[rows, :] += dot(prob.astype(jnp.bfloat16), grad, NN)
            grad_prob = dot(value_s[rows, :], grad, NT)
            grad_score = (prob * (grad_prob - delta)).astype(jnp.bfloat16)
            key_grad_s[rows, :] += dot(grad_score, query, NN)
            return query_grad + dot(key_s[:, rows], grad_score, NN)

        query_grad = lax.fori_loop(
            low_ref[i], last + 1, step, jnp.zeros((128, BLOCK), jnp.float32)
        )
        query_grad = (query_grad * SCALE).T.astype(jnp.bfloat16)
        query_ref[pl.ds(2 * i, 2)] = query_grad.reshape(2, 128, 128)
        return 0

    lax.fori_loop(0, tokens // BLOCK, query_block, 0)
    shape = keep_ref.shape

    @pl.when(even)
    def _():
        keep_ref[...] = (key_grad_s[...] * SCALE).astype(jnp.bfloat16).reshape(shape)
        send_ref[...] = value_grad_s[...].astype(jnp.bfloat16).reshape(shape)

    @pl.when(jnp.logical_not(even))
    def _():
        keep_ref[...] = value_grad_s[...].astype(jnp.bfloat16).reshape(shape)
        send_ref[...] = (key_grad_s[...] * SCALE).astype(jnp.bfloat16).reshape(shape)


def local(queries, keys, values, grad_out, readout, segments, loss_mask, labels):
    rows, heads, depth = queries.shape
    devices = lax.axis_size("context")
    index = lax.axis_index("context")
    clusters = [list(range(s, s + heads)) for s in range(0, devices, heads)]
    many = len(clusters) > 1
    halo = WINDOW if many else 0
    tokens = rows * heads
    key_tokens = tokens + halo
    pairs = [(i, i ^ 1) for i in range(devices)]
    bf16, f32 = jnp.bfloat16, jnp.float32

    def exchange(array):
        return lax.all_to_all(
            array, "context", 0, 0, tiled=True, axis_index_groups=clusters if many else None
        )

    def swap(array):
        return lax.ppermute(array, "context", pairs)

    pair = jnp.stack([keys, values], axis=2).reshape(rows, heads, depth)
    flags = jnp.stack([segments, loss_mask, labels]).astype(bf16)
    flags = jnp.pad(flags, ((0, AUX - 3), (0, 0)))
    message = jnp.concatenate(
        [
            jnp.transpose(queries, (1, 0, 2)),
            jnp.transpose(pair, (1, 0, 2)),
            jnp.broadcast_to(flags[None], (heads, AUX, depth)),
        ],
        axis=1,
    )
    message = exchange(message)
    later, message = lax.optimization_barrier((jnp.transpose(grad_out, (1, 0, 2)), message))
    grad = exchange(later)
    own = message[:, rows : 2 * rows]
    other = swap(own)
    flags = message[:, 2 * rows :]
    seg = flags[:, 0].astype(jnp.int32)
    flag = jnp.stack([flags[:, 1], flags[:, 2]]).astype(f32)
    if many:
        ahead = [(i, i + heads) for i in range(devices - heads)]
        blocks = halo // rows
        far = lax.ppermute((own[-blocks:], other[-blocks:], flags[-blocks:, 0]), "context", ahead)
        own = jnp.concatenate([far[0], own], axis=0)
        other = jnp.concatenate([far[1], other], axis=0)
        far_seg = jnp.where(index < heads, -1, far[2].astype(jnp.int32))
        seg = jnp.concatenate([far_seg, seg], axis=0)

    vmem = pl.BlockSpec(memory_space=pltpu.VMEM)
    smem = pl.BlockSpec(memory_space=pltpu.SMEM)
    count = tokens // BLOCK
    reach = WINDOW // BLOCK + 1
    where = jnp.reshape(index, (1,)).astype(jnp.int32)
    prob, out, inverse, reward, low = pl.pallas_call(
        functools.partial(forward_kernel, halo),
        out_shape=(
            jax.ShapeDtypeStruct((count, reach, BLOCK, BLOCK), bf16),
            jax.ShapeDtypeStruct((depth, tokens), f32),
            jax.ShapeDtypeStruct((count, BLOCK), f32),
            jax.ShapeDtypeStruct((heads, rows), f32),
            jax.ShapeDtypeStruct((count,), jnp.int32),
        ),
        in_specs=[smem] + [vmem] * 5,
        out_specs=(vmem, vmem, vmem, vmem, smem),
        scratch_shapes=[
            pltpu.VMEM((key_tokens, depth), bf16),
            pltpu.VMEM((depth, key_tokens), bf16),
            pltpu.VMEM((heads, rows), jnp.int32),
            pltpu.VMEM((reach, BLOCK, BLOCK), f32),
        ],
        compiler_params=pltpu.CompilerParams(vmem_limit_bytes=40 << 20),
        cost_estimate=pl.CostEstimate(
            flops=4 * BLOCK * BLOCK * depth * count * reach,
            bytes_accessed=16 << 20,
            transcendentals=BLOCK * BLOCK * count * reach,
        ),
        name="attention_forward",
    )(where, message, own, other, seg, readout)

    for step in (1, 2, 4, 8):
        reward = reward + lax.ppermute(reward, "context", [(i, i ^ step) for i in range(devices)])

    query_grad, keep, send = pl.pallas_call(
        functools.partial(backward_kernel, halo),
        out_shape=(
            jax.ShapeDtypeStruct((heads, rows, depth), bf16),
            jax.ShapeDtypeStruct((key_tokens // rows, rows, depth), bf16),
            jax.ShapeDtypeStruct((key_tokens // rows, rows, depth), bf16),
        ),
        in_specs=[smem, smem] + [vmem] * 10,
        out_specs=(vmem, vmem, vmem),
        scratch_shapes=[
            pltpu.VMEM((depth, key_tokens), bf16),
            pltpu.VMEM((key_tokens, depth), bf16),
            pltpu.VMEM((heads, rows, depth), bf16),
            pltpu.VMEM((count, BLOCK), f32),
            pltpu.VMEM((depth, tokens), f32),
            pltpu.VMEM((key_tokens, depth), f32),
            pltpu.VMEM((key_tokens, depth), f32),
        ],
        compiler_params=pltpu.CompilerParams(vmem_limit_bytes=40 << 20),
        cost_estimate=pl.CostEstimate(
            flops=8 * BLOCK * BLOCK * depth * count * reach,
            bytes_accessed=16 << 20,
            transcendentals=0,
        ),
        name="attention_backward",
    )(where, low, message, own, other, grad, readout, reward, flag, prob, out, inverse)

    total = keep.astype(f32) + swap(send).astype(f32)
    if many:
        behind = [(i + heads, i) for i in range(devices - heads)]
        back = lax.ppermute(total[:blocks].astype(bf16), "context", behind)
        total = total[blocks:]
        total = total + jnp.pad(
            back.astype(f32), ((heads - blocks, 0), (0, 0), (0, 0))
        )
    home = exchange(jnp.concatenate([query_grad, total.astype(bf16)], axis=1))
    home = jnp.transpose(home, (1, 0, 2))
    return home[:rows], home[rows:, 0::2], home[rows:, 1::2]


def solution(mesh):
    sharded = P(("groups", "context"))
    return jax.shard_map(
        local,
        mesh=mesh,
        in_specs=(sharded,) * 4 + (P(),) + (sharded,) * 3,
        out_specs=(sharded,) * 3,
        check_vma=False,
    )
```

```python
import functools
import math

import jax
import jax.numpy as jnp
from jax import lax
from jax.experimental import pallas as pl
from jax.experimental.pallas import tpu as pltpu
from jax.sharding import PartitionSpec as P

WINDOW = 1024
SCALE = 168.0 ** (-0.5)
LOG2E = math.log2(math.e)
NEGATIVE = -1e30
BLOCK = 256
AUX = 8
REACH = WINDOW // BLOCK + 1
VMEM = pl.BlockSpec(memory_space=pltpu.VMEM)
SMEM = pl.BlockSpec(memory_space=pltpu.SMEM)
HBM = pl.BlockSpec(memory_space=pltpu.HBM)
NT = (((1,), (1,)), ((), ()))
NN = (((1,), (0,)), ((), ()))


def dot(a, b, dims):
    return lax.dot_general(a, b, dims, preferred_element_type=jnp.float32)


def starts_of(seg_all, halo):
    return [jnp.sum(jnp.where(seg_all < s, 1, 0)) for s in range(0 if halo else 1, 4)]


def begin_of(starts, token):
    begin = jnp.zeros_like(token)
    for start in starts:
        begin = jnp.maximum(begin, jnp.where(start <= token, start, 0))
    return jnp.maximum(begin, token - (WINDOW - 1))


def by_reach(count, body):
    for n in range(1, REACH + 1):
        pl.when(count == n)(functools.partial(body, n))


def chunk(n):
    return pl.ds(n * BLOCK, BLOCK)


def forward_kernel(
    halo, index_ref, message_ref, own_ref, other_ref, seg_ref, readout_ref,
    prob_ref, inverse_ref, reward_ref, low_ref,
    key_s, side_s, bound_s, prob_s, sems,
):
    heads, tokens = message_ref.shape[0], message_ref.shape[0] * 128
    key_blocks = own_ref.shape[0]
    shift = halo // BLOCK
    index = index_ref[0]
    head = lax.rem(index, heads)
    even = lax.rem(index, 2) == 0
    low_bits = jnp.bfloat16

    weights = jnp.broadcast_to(readout_ref[pl.ds(head, 1), :], (8, 128))
    part = lax.broadcasted_iota(jnp.int32, (8, 128), 0)
    high = weights.astype(low_bits).astype(jnp.float32)
    middle = (weights - high).astype(low_bits).astype(jnp.float32)
    rest = weights - high - middle
    split = jnp.where(part == 0, high, jnp.where(part == 1, middle, rest))
    split = jnp.where(part < 3, split, 0.0).astype(low_bits)
    side = lax.broadcasted_iota(jnp.int32, (8, 128), 0)

    def place(keys, values):
        for s in range(key_blocks):
            key_s[s * 128 : (s + 1) * 128, :] = keys[s]
            worth = jnp.sum(dot(split, values[s], NT), axis=0, keepdims=True)
            worth_high = worth.astype(low_bits).astype(jnp.float32)
            lines = jnp.where(side == 0, worth_high, jnp.where(side == 1, worth - worth_high, 0.0))
            side_s[:, s * 128 : (s + 1) * 128] = jnp.where(side == 2, 1.0, lines).astype(low_bits)

    @pl.when(even)
    def _():
        place(own_ref, other_ref)

    @pl.when(jnp.logical_not(even))
    def _():
        place(other_ref, own_ref)

    starts = starts_of(seg_ref[...], halo)
    token = halo + lax.broadcasted_iota(jnp.int32, (tokens // BLOCK, BLOCK), 0) * BLOCK
    token = token + lax.broadcasted_iota(jnp.int32, (tokens // BLOCK, BLOCK), 1)
    bound_s[...] = begin_of(starts, token)
    key_iota = lax.broadcasted_iota(jnp.int32, (BLOCK, BLOCK), 0)
    query_iota = lax.broadcasted_iota(jnp.int32, (BLOCK, BLOCK), 1)

    def copy(i):
        return pltpu.make_async_copy(prob_s.at[i], prob_ref.at[i], sems.at[i])

    def query_block(i, _):
        first = lax.div(begin_of(starts, halo + i * BLOCK), BLOCK)
        low_ref[i] = first

        def body(n):
            query = message_ref[pl.ds(2 * i, 2), 0:128, :].reshape(BLOCK, 128)
            bound = bound_s[pl.ds(i, 1), :] - first * BLOCK
            scores, tops = [], []
            for j in range(n):
                rows = pl.ds(pl.multiple_of((first + j) * BLOCK, BLOCK), BLOCK)
                valid = key_iota >= bound - j * BLOCK
                if j == n - 1:
                    valid = valid & (key_iota <= query_iota)
                score = jnp.where(valid, dot(key_s[rows, :], query, NT), NEGATIVE)
                scores.append(score)
                tops.append(jnp.max(score.reshape(BLOCK // 8, 8, BLOCK), axis=0))
            top = jnp.max(functools.reduce(jnp.maximum, tops), axis=0, keepdims=True)
            sums = jnp.zeros((8, BLOCK), jnp.float32)
            for j in range(n):
                prob = jnp.exp2((scores[j] - top) * (SCALE * LOG2E)).astype(low_bits)
                prob_s[i, chunk(j), :] = prob
                columns = pl.ds(pl.multiple_of((first + j) * BLOCK, BLOCK), BLOCK)
                sums = sums + dot(side_s[:, columns], prob, NN)
            inverse = 1.0 / sums[2:3]
            reward = (sums[0:1] + sums[1:2]) * inverse
            for half in range(2):
                lanes = slice(half * 128, (half + 1) * 128)
                inverse_ref[pl.ds(2 * i + half, 1), :] = inverse[:, lanes]
                reward_ref[pl.ds(2 * i + half, 1), :] = reward[:, lanes]

        by_reach(i + shift + 1 - first, body)
        copy(i).start()
        return 0

    lax.fori_loop(0, tokens // BLOCK, query_block, 0)

    def finish(i, _):
        copy(i).wait()
        return 0

    lax.fori_loop(0, tokens // BLOCK, finish, 0)


def backward_kernel(
    halo, index_ref, low_ref, message_ref, own_ref, other_ref, grad_ref, readout_ref, reward_ref,
    flag_ref, inverse_ref, prob_ref,
    query_ref, keep_ref, send_ref,
    key_s, value_s, grad_s, scaled_s, query_s, prob_s, key_grad_s, value_grad_s, sems,
):
    heads, tokens = message_ref.shape[0], message_ref.shape[0] * 128
    key_blocks = own_ref.shape[0]
    shift = halo // BLOCK
    index = index_ref[0]
    head = lax.rem(index, heads)
    even = lax.rem(index, 2) == 0

    def copy(i):
        return pltpu.make_async_copy(prob_ref.at[i], prob_s.at[i], sems.at[i])

    for i in range(tokens // BLOCK):
        copy(i).start()

    def place(keys, values):
        for s in range(key_blocks):
            key_s[:, s * 128 : (s + 1) * 128] = keys[s].T
            value_s[s * 128 : (s + 1) * 128, :] = values[s]

    @pl.when(even)
    def _():
        place(own_ref, other_ref)

    @pl.when(jnp.logical_not(even))
    def _():
        place(other_ref, own_ref)

    live = flag_ref[0]
    probe = live * (jax.nn.sigmoid(reward_ref[...]) - flag_ref[1])
    live_t, probe_t, inverse_t = live.T, probe.T, inverse_ref[...].T
    weights = readout_ref[pl.ds(head, 1), :]
    for s in range(heads):
        grad = live_t[:, s : s + 1] * grad_ref[s].astype(jnp.float32)
        grad = (grad + probe_t[:, s : s + 1] * weights).astype(jnp.bfloat16)
        inverse = inverse_t[:, s : s + 1]
        grad_s[s] = grad
        scaled_s[s] = (grad.astype(jnp.float32) * inverse).astype(jnp.bfloat16)
        query_s[s] = (message_ref[s, 0:128, :].astype(jnp.float32) * inverse).astype(jnp.bfloat16)

    key_grad_s[...] = jnp.zeros_like(key_grad_s)
    value_grad_s[...] = jnp.zeros_like(value_grad_s)

    def query_block(i, _):
        first = low_ref[i]
        copy(i).wait()

        def body(n):
            grad = grad_s[pl.ds(2 * i, 2)].reshape(BLOCK, 128)
            scaled = scaled_s[pl.ds(2 * i, 2)].reshape(BLOCK, 128)
            query = query_s[pl.ds(2 * i, 2)].reshape(BLOCK, 128)
            inverse = jnp.concatenate(
                [inverse_ref[pl.ds(2 * i, 1), :], inverse_ref[pl.ds(2 * i + 1, 1), :]], axis=1
            )
            rows = [pl.ds(pl.multiple_of((first + j) * BLOCK, BLOCK), BLOCK) for j in range(n)]
            grad_probs = []
            delta = jnp.zeros((8, BLOCK), jnp.float32)
            for j in range(n):
                grad_prob = dot(value_s[rows[j], :], grad, NT)
                grad_probs.append(grad_prob)
                prob = prob_s[i, chunk(j), :].astype(jnp.float32)
                delta = delta + jnp.sum((prob * grad_prob).reshape(BLOCK // 8, 8, BLOCK), axis=0)
                value_grad_s[rows[j], :] += dot(prob_s[i, chunk(j), :], scaled, NN)
            delta = jnp.sum(delta, axis=0, keepdims=True) * inverse
            query_grad = jnp.zeros((128, BLOCK), jnp.float32)
            for j in range(n):
                prob = prob_s[i, chunk(j), :].astype(jnp.float32)
                grad_score = (prob * (grad_probs[j] - delta)).astype(jnp.bfloat16)
                key_grad_s[rows[j], :] += dot(grad_score, query, NN)
                query_grad = query_grad + dot(key_s[:, rows[j]], grad_score, NN)
            query_grad = (query_grad * (inverse * SCALE)).T.astype(jnp.bfloat16)
            query_ref[pl.ds(2 * i, 2)] = query_grad.reshape(2, 128, 128)

        by_reach(i + shift + 1 - first, body)
        return 0

    lax.fori_loop(0, tokens // BLOCK, query_block, 0)
    shape = keep_ref.shape

    @pl.when(even)
    def _():
        keep_ref[...] = (key_grad_s[...] * SCALE).astype(jnp.bfloat16).reshape(shape)
        send_ref[...] = value_grad_s[...].astype(jnp.bfloat16).reshape(shape)

    @pl.when(jnp.logical_not(even))
    def _():
        keep_ref[...] = value_grad_s[...].astype(jnp.bfloat16).reshape(shape)
        send_ref[...] = (key_grad_s[...] * SCALE).astype(jnp.bfloat16).reshape(shape)


def attention_forward(halo, where, message, own, other, seg, readout):
    heads, depth = message.shape[0], message.shape[2]
    key_tokens = own.shape[0] * own.shape[1]
    count = heads * own.shape[1] // BLOCK
    return pl.pallas_call(
        functools.partial(forward_kernel, halo),
        out_shape=(
            jax.ShapeDtypeStruct((count, REACH * BLOCK, BLOCK), jnp.bfloat16),
            jax.ShapeDtypeStruct((heads, own.shape[1]), jnp.float32),
            jax.ShapeDtypeStruct((heads, own.shape[1]), jnp.float32),
            jax.ShapeDtypeStruct((count,), jnp.int32),
        ),
        in_specs=[SMEM] + [VMEM] * 5,
        out_specs=(HBM, VMEM, VMEM, SMEM),
        scratch_shapes=[
            pltpu.VMEM((key_tokens, depth), jnp.bfloat16),
            pltpu.VMEM((8, key_tokens), jnp.bfloat16),
            pltpu.VMEM((count, BLOCK), jnp.int32),
            pltpu.VMEM((count, REACH * BLOCK, BLOCK), jnp.bfloat16),
            pltpu.SemaphoreType.DMA((count,)),
        ],
        compiler_params=pltpu.CompilerParams(vmem_limit_bytes=24 << 20),
        cost_estimate=pl.CostEstimate(
            flops=4 * BLOCK * BLOCK * depth * count * REACH,
            bytes_accessed=16 << 20,
            transcendentals=BLOCK * BLOCK * count * REACH,
        ),
        name="attention_forward",
    )(where, message, own, other, seg, readout)


def attention_backward(halo, where, low, message, own, other, grad, readout, reward, flag, inverse, prob):
    heads, depth = message.shape[0], message.shape[2]
    key_tokens = own.shape[0] * own.shape[1]
    count = heads * own.shape[1] // BLOCK
    return pl.pallas_call(
        functools.partial(backward_kernel, halo),
        out_shape=(
            jax.ShapeDtypeStruct(grad.shape, jnp.bfloat16),
            jax.ShapeDtypeStruct(own.shape, jnp.bfloat16),
            jax.ShapeDtypeStruct(own.shape, jnp.bfloat16),
        ),
        in_specs=[SMEM, SMEM] + [VMEM] * 8 + [HBM],
        out_specs=(VMEM, VMEM, VMEM),
        scratch_shapes=[
            pltpu.VMEM((depth, key_tokens), jnp.bfloat16),
            pltpu.VMEM((key_tokens, depth), jnp.bfloat16),
            pltpu.VMEM(grad.shape, jnp.bfloat16),
            pltpu.VMEM(grad.shape, jnp.bfloat16),
            pltpu.VMEM(grad.shape, jnp.bfloat16),
            pltpu.VMEM((count, REACH * BLOCK, BLOCK), jnp.bfloat16),
            pltpu.VMEM((key_tokens, depth), jnp.float32),
            pltpu.VMEM((key_tokens, depth), jnp.float32),
            pltpu.SemaphoreType.DMA((count,)),
        ],
        compiler_params=pltpu.CompilerParams(vmem_limit_bytes=24 << 20),
        cost_estimate=pl.CostEstimate(
            flops=8 * BLOCK * BLOCK * depth * count * REACH,
            bytes_accessed=16 << 20,
            transcendentals=0,
        ),
        name="attention_backward",
    )(where, low, message, own, other, grad, readout, reward, flag, inverse, prob)


def local(queries, keys, values, grad_out, readout, segments, loss_mask, labels):
    rows, heads, depth = queries.shape
    devices = lax.axis_size("context")
    index = lax.axis_index("context")
    clusters = [list(range(s, s + heads)) for s in range(0, devices, heads)]
    many = len(clusters) > 1
    halo = WINDOW if many else 0
    pairs = [(i, i ^ 1) for i in range(devices)]
    bf16, f32 = jnp.bfloat16, jnp.float32

    def exchange(array):
        return lax.all_to_all(
            array, "context", 0, 0, tiled=True, axis_index_groups=clusters if many else None
        )

    def swap(array):
        return lax.ppermute(array, "context", pairs)

    pair = jnp.stack([keys, values], axis=2).reshape(rows, heads, depth)
    flags = jnp.stack([segments, loss_mask, labels]).astype(bf16)
    flags = jnp.pad(flags, ((0, AUX - 3), (0, 0)))
    message = jnp.concatenate(
        [
            jnp.transpose(queries, (1, 0, 2)),
            jnp.transpose(pair, (1, 0, 2)),
            jnp.broadcast_to(flags[None], (heads, AUX, depth)),
        ],
        axis=1,
    )
    message = exchange(message)
    later, message = lax.optimization_barrier((jnp.transpose(grad_out, (1, 0, 2)), message))
    grad = exchange(later)
    own = message[:, rows : 2 * rows]
    other = swap(own)
    flags = message[:, 2 * rows :]
    seg = flags[:, 0].astype(jnp.int32)
    flag = jnp.stack([flags[:, 1], flags[:, 2]]).astype(f32)
    if many:
        ahead = [(i, i + heads) for i in range(devices - heads)]
        blocks = halo // rows
        far = lax.ppermute((own[-blocks:], other[-blocks:], flags[-blocks:, 0]), "context", ahead)
        own = jnp.concatenate([far[0], own], axis=0)
        other = jnp.concatenate([far[1], other], axis=0)
        far_seg = jnp.where(index < heads, -1, far[2].astype(jnp.int32))
        seg = jnp.concatenate([far_seg, seg], axis=0)

    where = jnp.reshape(index, (1,)).astype(jnp.int32)
    prob, inverse, reward, low = attention_forward(halo, where, message, own, other, seg, readout)

    for step in (1, 2, 4, 8):
        reward = reward + lax.ppermute(reward, "context", [(i, i ^ step) for i in range(devices)])

    query_grad, keep, send = attention_backward(
        halo, where, low, message, own, other, grad, readout, reward, flag, inverse, prob
    )
    total = keep.astype(f32) + swap(send).astype(f32)
    if many:
        behind = [(i + heads, i) for i in range(devices - heads)]
        back = lax.ppermute(total[:blocks].astype(bf16), "context", behind)
        total = total[blocks:]
        total = total + jnp.pad(
            back.astype(f32), ((heads - blocks, 0), (0, 0), (0, 0))
        )
    home = exchange(jnp.concatenate([query_grad, total.astype(bf16)], axis=1))
    home = jnp.transpose(home, (1, 0, 2))
    return home[:rows], home[rows:, 0::2], home[rows:, 1::2]


def solution(mesh):
    sharded = P(("groups", "context"))
    return jax.shard_map(
        local,
        mesh=mesh,
        in_specs=(sharded,) * 4 + (P(),) + (sharded,) * 3,
        out_specs=(sharded,) * 3,
        check_vma=False,
    )
```

```python
import functools
import math

import jax
import jax.numpy as jnp
from jax import lax
from jax.experimental import pallas as pl
from jax.experimental.pallas import tpu as pltpu
from jax.sharding import PartitionSpec as P

WINDOW = 1024
SCALE = 168.0 ** (-0.5)
LOG2E = math.log2(math.e)
NEGATIVE = -1e30
BLOCK = 256
AUX = 8
REACH = WINDOW // BLOCK + 1
VMEM = pl.BlockSpec(memory_space=pltpu.VMEM)
SMEM = pl.BlockSpec(memory_space=pltpu.SMEM)
NT = (((1,), (1,)), ((), ()))
NN = (((1,), (0,)), ((), ()))


def dot(a, b, dims):
    return lax.dot_general(a, b, dims, preferred_element_type=jnp.float32)


def starts_of(seg_all):
    return [jnp.sum(jnp.where(seg_all < s, 1, 0)) for s in range(4)]


def begin_of(starts, token):
    begin = token - (WINDOW - 1)
    for start in starts:
        begin = jnp.maximum(begin, jnp.where(start <= token, start, 0))
    return begin


def tokens_of(tokens, halo):
    shape = (tokens // BLOCK, BLOCK)
    row = lax.broadcasted_iota(jnp.int32, shape, 0)
    return halo + row * BLOCK + lax.broadcasted_iota(jnp.int32, shape, 1)


def rows_of(block):
    return pl.ds(pl.multiple_of(block * BLOCK, BLOCK), BLOCK)


def by_reach(count, body):
    for n in range(1, REACH + 1):
        pl.when(count == n)(functools.partial(body, n))


def forward_kernel(
    halo, index_ref, message_ref, own_ref, other_ref, seg_ref, readout_ref,
    total_ref, reward_ref, starts_ref,
    key_s, side_s, bound_s,
):
    heads, tokens = message_ref.shape[0], message_ref.shape[0] * 128
    key_blocks = own_ref.shape[0]
    shift = halo // BLOCK
    index = index_ref[0]
    head = lax.rem(index, heads)
    even = lax.rem(index, 2) == 0
    low_bits = jnp.bfloat16

    weights = jnp.broadcast_to(readout_ref[pl.ds(head, 1), :], (8, 128))
    part = lax.broadcasted_iota(jnp.int32, (8, 128), 0)
    high = weights.astype(low_bits).astype(jnp.float32)
    middle = (weights - high).astype(low_bits).astype(jnp.float32)
    rest = weights - high - middle
    split = jnp.where(part == 0, high, jnp.where(part == 1, middle, rest))
    split = jnp.where(part < 3, split, 0.0).astype(low_bits)
    side = lax.broadcasted_iota(jnp.int32, (8, 128), 0)

    def place(keys, values):
        for s in range(key_blocks):
            key_s[s * 128 : (s + 1) * 128, :] = keys[s]
            worth = jnp.sum(dot(split, values[s], NT), axis=0, keepdims=True)
            worth_high = worth.astype(low_bits).astype(jnp.float32)
            lines = jnp.where(side == 0, worth_high, jnp.where(side == 1, worth - worth_high, 0.0))
            side_s[:, s * 128 : (s + 1) * 128] = jnp.where(side == 2, 1.0, lines).astype(low_bits)

    @pl.when(even)
    def _():
        place(own_ref, other_ref)

    @pl.when(jnp.logical_not(even))
    def _():
        place(other_ref, own_ref)

    starts = starts_of(seg_ref[...])
    for n, start in enumerate(starts):
        starts_ref[n] = start
    bound_s[...] = begin_of(starts, tokens_of(tokens, halo))
    key_iota = lax.broadcasted_iota(jnp.int32, (BLOCK, BLOCK), 0)
    query_iota = lax.broadcasted_iota(jnp.int32, (BLOCK, BLOCK), 1)

    def query_block(i, _):
        first = lax.div(begin_of(starts, halo + i * BLOCK), BLOCK)

        def body(n):
            query = message_ref[pl.ds(2 * i, 2), 0:128, :].reshape(BLOCK, 128)
            bound = bound_s[pl.ds(i, 1), :] - first * BLOCK
            scores, tops = [], []
            for j in range(n):
                score = dot(key_s[rows_of(first + j), :], query, NT)
                valid = key_iota >= bound - j * BLOCK
                if j == n - 1:
                    valid = valid & (key_iota <= query_iota)
                score = jnp.where(valid, score, NEGATIVE)
                scores.append(score)
                tops.append(jnp.max(score.reshape(BLOCK // 8, 8, BLOCK), axis=0))
            top = jnp.max(functools.reduce(jnp.maximum, tops), axis=0, keepdims=True)
            sums = jnp.zeros((8, BLOCK), jnp.float32)
            for j in range(n):
                prob = jnp.exp2((scores[j] - top) * (SCALE * LOG2E)).astype(low_bits)
                sums = sums + dot(side_s[:, rows_of(first + j)], prob, NN)
            reward = (sums[0:1] + sums[1:2]) / sums[2:3]
            total_ref[pl.ds(i, 1), :] = top * (SCALE * LOG2E) + jnp.log2(sums[2:3])
            reward_ref[pl.ds(2 * i, 1), :] = reward[:, :128]
            reward_ref[pl.ds(2 * i + 1, 1), :] = reward[:, 128:]

        by_reach(i + shift + 1 - first, body)
        return 0

    lax.fori_loop(0, tokens // BLOCK, query_block, 0)


def backward_kernel(
    halo, index_ref, starts_ref, message_ref, own_ref, other_ref, grad_ref, readout_ref, reward_ref,
    flag_ref, total_ref,
    query_ref, keep_ref, send_ref,
    key_s, turned_s, value_s, grad_s, bound_s, key_grad_s, value_grad_s,
):
    heads, tokens = message_ref.shape[0], message_ref.shape[0] * 128
    key_blocks = own_ref.shape[0]
    shift = halo // BLOCK
    index = index_ref[0]
    head = lax.rem(index, heads)
    even = lax.rem(index, 2) == 0

    def place(keys, values):
        for s in range(key_blocks):
            key_s[s * 128 : (s + 1) * 128, :] = keys[s]
            turned_s[:, s * 128 : (s + 1) * 128] = keys[s].T
            value_s[s * 128 : (s + 1) * 128, :] = values[s]

    @pl.when(even)
    def _():
        place(own_ref, other_ref)

    @pl.when(jnp.logical_not(even))
    def _():
        place(other_ref, own_ref)

    live = flag_ref[0]
    probe = live * (jax.nn.sigmoid(reward_ref[...]) - flag_ref[1])
    live_t, probe_t = live.T, probe.T
    weights = readout_ref[pl.ds(head, 1), :]
    for s in range(heads):
        grad = live_t[:, s : s + 1] * grad_ref[s].astype(jnp.float32)
        grad_s[s] = (grad + probe_t[:, s : s + 1] * weights).astype(jnp.bfloat16)

    starts = [starts_ref[n] for n in range(4)]
    bound_s[...] = begin_of(starts, tokens_of(tokens, halo))
    key_iota = lax.broadcasted_iota(jnp.int32, (BLOCK, BLOCK), 0)
    query_iota = lax.broadcasted_iota(jnp.int32, (BLOCK, BLOCK), 1)
    if halo:
        key_grad_s[:halo, :] = jnp.zeros((halo, 128), jnp.float32)
        value_grad_s[:halo, :] = jnp.zeros((halo, 128), jnp.float32)

    def query_block(i, _):
        first = lax.div(begin_of(starts, halo + i * BLOCK), BLOCK)

        def body(n):
            grad = grad_s[pl.ds(2 * i, 2)].reshape(BLOCK, 128)
            query = message_ref[pl.ds(2 * i, 2), 0:128, :].reshape(BLOCK, 128)
            bound = bound_s[pl.ds(i, 1), :] - first * BLOCK
            total = total_ref[pl.ds(i, 1), :]
            probs, grad_probs = [], []
            delta = jnp.zeros((8, BLOCK), jnp.float32)
            for j in range(n):
                rows = rows_of(first + j)
                score = dot(key_s[rows, :], query, NT) * (SCALE * LOG2E) - total
                valid = key_iota >= bound - j * BLOCK
                if j == n - 1:
                    valid = valid & (key_iota <= query_iota)
                prob = jnp.exp2(jnp.where(valid, score, NEGATIVE))
                grad_prob = dot(value_s[rows, :], grad, NT)
                delta = delta + jnp.sum((prob * grad_prob).reshape(BLOCK // 8, 8, BLOCK), axis=0)
                value_grad = dot(prob.astype(jnp.bfloat16), grad, NN)
                if j == n - 1:
                    value_grad_s[rows, :] = value_grad
                else:
                    value_grad_s[rows, :] += value_grad
                probs.append(prob)
                grad_probs.append(grad_prob)
            delta = jnp.sum(delta, axis=0, keepdims=True)
            query_grad = jnp.zeros((128, BLOCK), jnp.float32)
            for j in range(n):
                rows = rows_of(first + j)
                grad_score = (probs[j] * (grad_probs[j] - delta)).astype(jnp.bfloat16)
                key_grad = dot(grad_score, query, NN)
                if j == n - 1:
                    key_grad_s[rows, :] = key_grad
                else:
                    key_grad_s[rows, :] += key_grad
                query_grad = query_grad + dot(turned_s[:, rows], grad_score, NN)
            query_grad = (query_grad * SCALE).T.astype(jnp.bfloat16)
            query_ref[pl.ds(2 * i, 2)] = query_grad.reshape(2, 128, 128)

        by_reach(i + shift + 1 - first, body)
        return 0

    lax.fori_loop(0, tokens // BLOCK, query_block, 0)
    shape = keep_ref.shape

    @pl.when(even)
    def _():
        keep_ref[...] = (key_grad_s[...] * SCALE).astype(jnp.bfloat16).reshape(shape)
        send_ref[...] = value_grad_s[...].astype(jnp.bfloat16).reshape(shape)

    @pl.when(jnp.logical_not(even))
    def _():
        keep_ref[...] = value_grad_s[...].astype(jnp.bfloat16).reshape(shape)
        send_ref[...] = (key_grad_s[...] * SCALE).astype(jnp.bfloat16).reshape(shape)


def attention_forward(halo, where, message, own, other, seg, readout):
    heads, depth = message.shape[0], message.shape[2]
    key_tokens = own.shape[0] * own.shape[1]
    count = heads * own.shape[1] // BLOCK
    return pl.pallas_call(
        functools.partial(forward_kernel, halo),
        out_shape=(
            jax.ShapeDtypeStruct((count, BLOCK), jnp.float32),
            jax.ShapeDtypeStruct((heads, own.shape[1]), jnp.float32),
            jax.ShapeDtypeStruct((4,), jnp.int32),
        ),
        in_specs=[SMEM] + [VMEM] * 5,
        out_specs=(VMEM, VMEM, SMEM),
        scratch_shapes=[
            pltpu.VMEM((key_tokens, depth), jnp.bfloat16),
            pltpu.VMEM((8, key_tokens), jnp.bfloat16),
            pltpu.VMEM((count, BLOCK), jnp.int32),
        ],
        compiler_params=pltpu.CompilerParams(vmem_limit_bytes=24 << 20),
        cost_estimate=pl.CostEstimate(
            flops=4 * BLOCK * BLOCK * depth * count * REACH,
            bytes_accessed=16 << 20,
            transcendentals=BLOCK * BLOCK * count * REACH,
        ),
        name="attention_forward",
    )(where, message, own, other, seg, readout)


def attention_backward(halo, where, starts, message, own, other, grad, readout, reward, flag, total):
    heads, depth = message.shape[0], message.shape[2]
    key_tokens = own.shape[0] * own.shape[1]
    count = heads * own.shape[1] // BLOCK
    return pl.pallas_call(
        functools.partial(backward_kernel, halo),
        out_shape=(
            jax.ShapeDtypeStruct(grad.shape, jnp.bfloat16),
            jax.ShapeDtypeStruct(own.shape, jnp.bfloat16),
            jax.ShapeDtypeStruct(own.shape, jnp.bfloat16),
        ),
        in_specs=[SMEM, SMEM] + [VMEM] * 8,
        out_specs=(VMEM, VMEM, VMEM),
        scratch_shapes=[
            pltpu.VMEM((key_tokens, depth), jnp.bfloat16),
            pltpu.VMEM((depth, key_tokens), jnp.bfloat16),
            pltpu.VMEM((key_tokens, depth), jnp.bfloat16),
            pltpu.VMEM(grad.shape, jnp.bfloat16),
            pltpu.VMEM((count, BLOCK), jnp.int32),
            pltpu.VMEM((key_tokens, depth), jnp.float32),
            pltpu.VMEM((key_tokens, depth), jnp.float32),
        ],
        compiler_params=pltpu.CompilerParams(vmem_limit_bytes=24 << 20),
        cost_estimate=pl.CostEstimate(
            flops=8 * BLOCK * BLOCK * depth * count * REACH,
            bytes_accessed=16 << 20,
            transcendentals=0,
        ),
        name="attention_backward",
    )(where, starts, message, own, other, grad, readout, reward, flag, total)


def local(queries, keys, values, grad_out, readout, segments, loss_mask, labels):
    rows, heads, depth = queries.shape
    devices = lax.axis_size("context")
    index = lax.axis_index("context")
    clusters = [list(range(s, s + heads)) for s in range(0, devices, heads)]
    many = len(clusters) > 1
    halo = WINDOW if many else 0
    pairs = [(i, i ^ 1) for i in range(devices)]
    bf16, f32 = jnp.bfloat16, jnp.float32

    def exchange(array):
        return lax.all_to_all(
            array, "context", 0, 0, tiled=True, axis_index_groups=clusters if many else None
        )

    def swap(array):
        return lax.ppermute(array, "context", pairs)

    pair = jnp.stack([keys, values], axis=2).reshape(rows, heads, depth)
    flags = jnp.stack([segments, loss_mask, labels]).astype(bf16)
    flags = jnp.pad(flags, ((0, AUX - 3), (0, 0)))
    message = jnp.concatenate(
        [
            jnp.transpose(queries, (1, 0, 2)),
            jnp.transpose(pair, (1, 0, 2)),
            jnp.broadcast_to(flags[None], (heads, AUX, depth)),
        ],
        axis=1,
    )
    message = exchange(message)
    later, message = lax.optimization_barrier((jnp.transpose(grad_out, (1, 0, 2)), message))
    grad = exchange(later)
    own = message[:, rows : 2 * rows]
    other = swap(own)
    flags = message[:, 2 * rows :]
    seg = flags[:, 0].astype(jnp.int32)
    flag = jnp.stack([flags[:, 1], flags[:, 2]]).astype(f32)
    if many:
        ahead = [(i, i + heads) for i in range(devices - heads)]
        blocks = halo // rows
        far = lax.ppermute((own[-blocks:], other[-blocks:], flags[-blocks:, 0]), "context", ahead)
        own = jnp.concatenate([far[0], own], axis=0)
        other = jnp.concatenate([far[1], other], axis=0)
        far_seg = jnp.where(index < heads, -1, far[2].astype(jnp.int32))
        seg = jnp.concatenate([far_seg, seg], axis=0)

    where = jnp.reshape(index, (1,)).astype(jnp.int32)
    total, reward, starts = attention_forward(halo, where, message, own, other, seg, readout)

    for step in (1, 2, 4, 8):
        reward = reward + lax.ppermute(reward, "context", [(i, i ^ step) for i in range(devices)])

    query_grad, keep, send = attention_backward(
        halo, where, starts, message, own, other, grad, readout, reward, flag, total
    )
    total = keep.astype(f32) + swap(send).astype(f32)
    if many:
        behind = [(i + heads, i) for i in range(devices - heads)]
        back = lax.ppermute(total[:blocks].astype(bf16), "context", behind)
        total = total[blocks:]
        total = total + jnp.pad(
            back.astype(f32), ((heads - blocks, 0), (0, 0), (0, 0))
        )
    home = exchange(jnp.concatenate([query_grad, total.astype(bf16)], axis=1))
    home = jnp.transpose(home, (1, 0, 2))
    return home[:rows], home[rows:, 0::2], home[rows:, 1::2]


def solution(mesh):
    sharded = P(("groups", "context"))
    return jax.shard_map(
        local,
        mesh=mesh,
        in_specs=(sharded,) * 4 + (P(),) + (sharded,) * 3,
        out_specs=(sharded,) * 3,
        check_vma=False,
    )
```

```python
import functools
import math

import jax
import jax.numpy as jnp
from jax import lax
from jax.experimental import pallas as pl
from jax.experimental.pallas import tpu as pltpu
from jax.sharding import PartitionSpec as P

WINDOW = 1024
SCALE = 168.0 ** (-0.5)
LOG2E = math.log2(math.e)
NEGATIVE = -1e30
BLOCK = 256
AUX = 8
QUERIES = 2 * BLOCK
REACH = (WINDOW + QUERIES) // BLOCK
VMEM = pl.BlockSpec(memory_space=pltpu.VMEM)
SMEM = pl.BlockSpec(memory_space=pltpu.SMEM)
NT = (((1,), (1,)), ((), ()))
NN = (((1,), (0,)), ((), ()))


def dot(a, b, dims):
    return lax.dot_general(a, b, dims, preferred_element_type=jnp.float32)


def starts_of(seg_all):
    return [jnp.sum(jnp.where(seg_all < s, 1, 0)) for s in range(4)]


def begin_of(starts, token):
    begin = token - (WINDOW - 1)
    for start in starts:
        begin = jnp.maximum(begin, jnp.where(start <= token, start, 0))
    return begin


def tokens_of(tokens, halo):
    shape = (tokens // QUERIES, QUERIES)
    row = lax.broadcasted_iota(jnp.int32, shape, 0)
    return halo + row * QUERIES + lax.broadcasted_iota(jnp.int32, shape, 1)


def rows_of(block):
    return pl.ds(pl.multiple_of(block * BLOCK, BLOCK), BLOCK)


def by_reach(count, body):
    for n in range(2, REACH + 1):
        pl.when(count == n)(functools.partial(body, n))


def late(j, n):
    return slice(BLOCK, QUERIES) if j == n - 1 else slice(0, QUERIES)


def valid_of(key_iota, causal, bound, j, n):
    span = late(j, n)
    valid = key_iota[:, span] >= bound[:, span] - j * BLOCK
    if j == n - 1:
        return valid & causal[:, :BLOCK]
    return valid & causal if j == n - 2 else valid


def fold(parts, combine, reduce):
    if reduce is not None:
        parts = [reduce(p.reshape(p.shape[0] // 8, 8, p.shape[1]), axis=0) for p in parts]
    whole = functools.reduce(combine, parts[:-1])
    return jnp.concatenate([whole[:, :BLOCK], combine(whole[:, BLOCK:], parts[-1])], axis=1)


def forward_kernel(
    halo, index_ref, message_ref, own_ref, other_ref, seg_ref, readout_ref,
    total_ref, reward_ref, starts_ref,
    key_s, side_s, bound_s,
):
    heads, tokens = message_ref.shape[0], message_ref.shape[0] * 128
    key_blocks = own_ref.shape[0]
    shift = halo // BLOCK
    index = index_ref[0]
    head = lax.rem(index, heads)
    even = lax.rem(index, 2) == 0
    low_bits = jnp.bfloat16

    weights = jnp.broadcast_to(readout_ref[pl.ds(head, 1), :], (8, 128))
    part = lax.broadcasted_iota(jnp.int32, (8, 128), 0)
    high = weights.astype(low_bits).astype(jnp.float32)
    middle = (weights - high).astype(low_bits).astype(jnp.float32)
    rest = weights - high - middle
    split = jnp.where(part == 0, high, jnp.where(part == 1, middle, rest))
    split = jnp.where(part < 3, split, 0.0).astype(low_bits)
    side = lax.broadcasted_iota(jnp.int32, (8, 128), 0)

    def place(keys, values):
        for s in range(key_blocks):
            key_s[s * 128 : (s + 1) * 128, :] = keys[s]
            worth = jnp.sum(dot(split, values[s], NT), axis=0, keepdims=True)
            worth_high = worth.astype(low_bits).astype(jnp.float32)
            lines = jnp.where(side == 0, worth_high, jnp.where(side == 1, worth - worth_high, 0.0))
            side_s[:, s * 128 : (s + 1) * 128] = jnp.where(side == 2, 1.0, lines).astype(low_bits)

    @pl.when(even)
    def _():
        place(own_ref, other_ref)

    @pl.when(jnp.logical_not(even))
    def _():
        place(other_ref, own_ref)

    starts = starts_of(seg_ref[...])
    for n, start in enumerate(starts):
        starts_ref[n] = start
    bound_s[...] = begin_of(starts, tokens_of(tokens, halo))
    key_iota = lax.broadcasted_iota(jnp.int32, (BLOCK, QUERIES), 0)
    query_iota = lax.broadcasted_iota(jnp.int32, (BLOCK, QUERIES), 1)
    causal = key_iota <= query_iota

    def query_block(i, _):
        first = lax.div(begin_of(starts, halo + i * QUERIES), BLOCK)

        def body(n):
            query = message_ref[pl.ds(4 * i, 4), 0:128, :].reshape(QUERIES, 128)
            bound = bound_s[pl.ds(i, 1), :] - first * BLOCK
            scores = []
            for j in range(n):
                span = late(j, n)
                score = dot(key_s[rows_of(first + j), :], query[span], NT)
                scores.append(jnp.where(valid_of(key_iota, causal, bound, j, n), score, NEGATIVE))
            top = jnp.max(fold(scores, jnp.maximum, jnp.max), axis=0, keepdims=True)
            sums = []
            for j in range(n):
                prob = jnp.exp2((scores[j] - top[:, late(j, n)]) * (SCALE * LOG2E))
                sums.append(dot(side_s[:, rows_of(first + j)], prob.astype(low_bits), NN))
            sums = fold(sums, jnp.add, None)
            reward = (sums[0:1] + sums[1:2]) / sums[2:3]
            total_ref[pl.ds(i, 1), :] = top * (SCALE * LOG2E) + jnp.log2(sums[2:3])
            for part in range(4):
                reward_ref[pl.ds(4 * i + part, 1), :] = reward[:, part * 128 : (part + 1) * 128]

        by_reach(2 * i + 2 + shift - first, body)
        return 0

    lax.fori_loop(0, tokens // QUERIES, query_block, 0)


def backward_kernel(
    halo, index_ref, starts_ref, message_ref, own_ref, other_ref, grad_ref, readout_ref, reward_ref,
    flag_ref, total_ref,
    query_ref, keep_ref, send_ref,
    key_s, turned_s, value_s, grad_s, bound_s, key_grad_s, value_grad_s,
):
    heads, tokens = message_ref.shape[0], message_ref.shape[0] * 128
    key_blocks = own_ref.shape[0]
    shift = halo // BLOCK
    index = index_ref[0]
    head = lax.rem(index, heads)
    even = lax.rem(index, 2) == 0

    def place(keys, values):
        for s in range(key_blocks):
            key_s[s * 128 : (s + 1) * 128, :] = keys[s]
            turned_s[:, s * 128 : (s + 1) * 128] = keys[s].T
            value_s[s * 128 : (s + 1) * 128, :] = values[s]

    @pl.when(even)
    def _():
        place(own_ref, other_ref)

    @pl.when(jnp.logical_not(even))
    def _():
        place(other_ref, own_ref)

    live = flag_ref[0]
    probe = live * (jax.nn.sigmoid(reward_ref[...]) - flag_ref[1])
    live_t, probe_t = live.T, probe.T
    weights = readout_ref[pl.ds(head, 1), :]
    for s in range(heads):
        grad = live_t[:, s : s + 1] * grad_ref[s].astype(jnp.float32)
        grad_s[s] = (grad + probe_t[:, s : s + 1] * weights).astype(jnp.bfloat16)

    starts = [starts_ref[n] for n in range(4)]
    bound_s[...] = begin_of(starts, tokens_of(tokens, halo))
    key_iota = lax.broadcasted_iota(jnp.int32, (BLOCK, QUERIES), 0)
    query_iota = lax.broadcasted_iota(jnp.int32, (BLOCK, QUERIES), 1)
    causal = key_iota <= query_iota
    if halo:
        key_grad_s[:halo, :] = jnp.zeros((halo, 128), jnp.float32)
        value_grad_s[:halo, :] = jnp.zeros((halo, 128), jnp.float32)

    def query_block(i, _):
        first = lax.div(begin_of(starts, halo + i * QUERIES), BLOCK)

        def body(n):
            grad = grad_s[pl.ds(4 * i, 4)].reshape(QUERIES, 128)
            query = message_ref[pl.ds(4 * i, 4), 0:128, :].reshape(QUERIES, 128)
            bound = bound_s[pl.ds(i, 1), :] - first * BLOCK
            total = total_ref[pl.ds(i, 1), :]
            probs, grad_probs, deltas = [], [], []
            for j in range(n):
                rows, span = rows_of(first + j), late(j, n)
                score = dot(key_s[rows, :], query[span], NT) * (SCALE * LOG2E) - total[:, span]
                valid = valid_of(key_iota, causal, bound, j, n)
                prob = jnp.exp2(jnp.where(valid, score, NEGATIVE))
                grad_prob = dot(value_s[rows, :], grad[span], NT)
                deltas.append(prob * grad_prob)
                value_grad = dot(prob.astype(jnp.bfloat16), grad[span], NN)
                if j >= n - 2:
                    value_grad_s[rows, :] = value_grad
                else:
                    value_grad_s[rows, :] += value_grad
                probs.append(prob)
                grad_probs.append(grad_prob)
            delta = jnp.sum(fold(deltas, jnp.add, jnp.sum), axis=0, keepdims=True)
            query_grads = []
            for j in range(n):
                rows, span = rows_of(first + j), late(j, n)
                grad_score = (probs[j] * (grad_probs[j] - delta[:, span])).astype(jnp.bfloat16)
                key_grad = dot(grad_score, query[span], NN)
                if j >= n - 2:
                    key_grad_s[rows, :] = key_grad
                else:
                    key_grad_s[rows, :] += key_grad
                query_grads.append(dot(turned_s[:, rows], grad_score, NN))
            query_grad = (fold(query_grads, jnp.add, None) * SCALE).T.astype(jnp.bfloat16)
            query_ref[pl.ds(4 * i, 4)] = query_grad.reshape(4, 128, 128)

        by_reach(2 * i + 2 + shift - first, body)
        return 0

    lax.fori_loop(0, tokens // QUERIES, query_block, 0)
    shape = keep_ref.shape

    @pl.when(even)
    def _():
        keep_ref[...] = (key_grad_s[...] * SCALE).astype(jnp.bfloat16).reshape(shape)
        send_ref[...] = value_grad_s[...].astype(jnp.bfloat16).reshape(shape)

    @pl.when(jnp.logical_not(even))
    def _():
        keep_ref[...] = value_grad_s[...].astype(jnp.bfloat16).reshape(shape)
        send_ref[...] = (key_grad_s[...] * SCALE).astype(jnp.bfloat16).reshape(shape)


def attention_forward(halo, where, message, own, other, seg, readout):
    heads, depth = message.shape[0], message.shape[2]
    key_tokens = own.shape[0] * own.shape[1]
    count = message.shape[0] * 128 // QUERIES
    return pl.pallas_call(
        functools.partial(forward_kernel, halo),
        out_shape=(
            jax.ShapeDtypeStruct((count, QUERIES), jnp.float32),
            jax.ShapeDtypeStruct((heads, own.shape[1]), jnp.float32),
            jax.ShapeDtypeStruct((4,), jnp.int32),
        ),
        in_specs=[SMEM] + [VMEM] * 5,
        out_specs=(VMEM, VMEM, SMEM),
        scratch_shapes=[
            pltpu.VMEM((key_tokens, depth), jnp.bfloat16),
            pltpu.VMEM((8, key_tokens), jnp.bfloat16),
            pltpu.VMEM((count, QUERIES), jnp.int32),
        ],
        compiler_params=pltpu.CompilerParams(vmem_limit_bytes=24 << 20),
        cost_estimate=pl.CostEstimate(
            flops=4 * BLOCK * QUERIES * depth * count * REACH,
            bytes_accessed=16 << 20,
            transcendentals=BLOCK * QUERIES * count * REACH,
        ),
        name="attention_forward",
    )(where, message, own, other, seg, readout)


def attention_backward(halo, where, starts, message, own, other, grad, readout, reward, flag, total):
    heads, depth = message.shape[0], message.shape[2]
    key_tokens = own.shape[0] * own.shape[1]
    count = message.shape[0] * 128 // QUERIES
    return pl.pallas_call(
        functools.partial(backward_kernel, halo),
        out_shape=(
            jax.ShapeDtypeStruct(grad.shape, jnp.bfloat16),
            jax.ShapeDtypeStruct(own.shape, jnp.bfloat16),
            jax.ShapeDtypeStruct(own.shape, jnp.bfloat16),
        ),
        in_specs=[SMEM, SMEM] + [VMEM] * 8,
        out_specs=(VMEM, VMEM, VMEM),
        scratch_shapes=[
            pltpu.VMEM((key_tokens, depth), jnp.bfloat16),
            pltpu.VMEM((depth, key_tokens), jnp.bfloat16),
            pltpu.VMEM((key_tokens, depth), jnp.bfloat16),
            pltpu.VMEM(grad.shape, jnp.bfloat16),
            pltpu.VMEM((count, QUERIES), jnp.int32),
            pltpu.VMEM((key_tokens, depth), jnp.float32),
            pltpu.VMEM((key_tokens, depth), jnp.float32),
        ],
        compiler_params=pltpu.CompilerParams(vmem_limit_bytes=24 << 20),
        cost_estimate=pl.CostEstimate(
            flops=10 * BLOCK * QUERIES * depth * count * REACH,
            bytes_accessed=16 << 20,
            transcendentals=0,
        ),
        name="attention_backward",
    )(where, starts, message, own, other, grad, readout, reward, flag, total)


def local(queries, keys, values, grad_out, readout, segments, loss_mask, labels):
    rows, heads, depth = queries.shape
    devices = lax.axis_size("context")
    index = lax.axis_index("context")
    clusters = [list(range(s, s + heads)) for s in range(0, devices, heads)]
    many = len(clusters) > 1
    halo = WINDOW if many else 0
    pairs = [(i, i ^ 1) for i in range(devices)]
    bf16, f32 = jnp.bfloat16, jnp.float32

    def exchange(array):
        return lax.all_to_all(
            array, "context", 0, 0, tiled=True, axis_index_groups=clusters if many else None
        )

    def swap(array):
        return lax.ppermute(array, "context", pairs)

    pair = jnp.stack([keys, values], axis=2).reshape(rows, heads, depth)
    flags = jnp.stack([segments, loss_mask, labels]).astype(bf16)
    flags = jnp.pad(flags, ((0, AUX - 3), (0, 0)))
    message = jnp.concatenate(
        [
            jnp.transpose(queries, (1, 0, 2)),
            jnp.transpose(pair, (1, 0, 2)),
            jnp.broadcast_to(flags[None], (heads, AUX, depth)),
        ],
        axis=1,
    )
    message = exchange(message)
    later, message = lax.optimization_barrier((jnp.transpose(grad_out, (1, 0, 2)), message))
    grad = exchange(later)
    own = message[:, rows : 2 * rows]
    other = swap(own)
    flags = message[:, 2 * rows :]
    seg = flags[:, 0].astype(jnp.int32)
    flag = jnp.stack([flags[:, 1], flags[:, 2]]).astype(f32)
    if many:
        ahead = [(i, i + heads) for i in range(devices - heads)]
        blocks = halo // rows
        far = lax.ppermute((own[-blocks:], other[-blocks:], flags[-blocks:, 0]), "context", ahead)
        own = jnp.concatenate([far[0], own], axis=0)
        other = jnp.concatenate([far[1], other], axis=0)
        far_seg = jnp.where(index < heads, -1, far[2].astype(jnp.int32))
        seg = jnp.concatenate([far_seg, seg], axis=0)

    where = jnp.reshape(index, (1,)).astype(jnp.int32)
    total, reward, starts = attention_forward(halo, where, message, own, other, seg, readout)

    for step in (1, 2, 4, 8):
        reward = reward + lax.ppermute(reward, "context", [(i, i ^ step) for i in range(devices)])

    query_grad, keep, send = attention_backward(
        halo, where, starts, message, own, other, grad, readout, reward, flag, total
    )
    total = keep.astype(f32) + swap(send).astype(f32)
    if many:
        behind = [(i + heads, i) for i in range(devices - heads)]
        back = lax.ppermute(total[:blocks].astype(bf16), "context", behind)
        total = total[blocks:]
        total = total + jnp.pad(
            back.astype(f32), ((heads - blocks, 0), (0, 0), (0, 0))
        )
    home = exchange(jnp.concatenate([query_grad, total.astype(bf16)], axis=1))
    home = jnp.transpose(home, (1, 0, 2))
    return home[:rows], home[rows:, 0::2], home[rows:, 1::2]


def solution(mesh):
    sharded = P(("groups", "context"))
    return jax.shard_map(
        local,
        mesh=mesh,
        in_specs=(sharded,) * 4 + (P(),) + (sharded,) * 3,
        out_specs=(sharded,) * 3,
        check_vma=False,
    )
```

```python
import functools
import math

import jax
import jax.numpy as jnp
from jax import lax
from jax.experimental import pallas as pl
from jax.experimental.pallas import tpu as pltpu
from jax.sharding import PartitionSpec as P

WINDOW = 1024
SCALE = 168.0 ** (-0.5)
LOG2E = math.log2(math.e)
NEGATIVE = -1e30
BLOCK = 256
AUX = 8
QUERIES = 2 * BLOCK
REACH = (WINDOW + QUERIES) // BLOCK
VMEM = pl.BlockSpec(memory_space=pltpu.VMEM)
ANY = pl.BlockSpec(memory_space=pl.ANY)
SMEM = pl.BlockSpec(memory_space=pltpu.SMEM)
NT = (((1,), (1,)), ((), ()))
NN = (((1,), (0,)), ((), ()))


def dot(a, b, dims):
    return lax.dot_general(a, b, dims, preferred_element_type=jnp.float32)


def starts_of(seg_all):
    return [jnp.sum(jnp.where(seg_all < s, 1, 0)) for s in range(4)]


def begin_of(starts, token):
    begin = token - (WINDOW - 1)
    for start in starts:
        begin = jnp.maximum(begin, jnp.where(start <= token, start, 0))
    return begin


def tokens_of(tokens, halo):
    shape = (tokens // QUERIES, QUERIES)
    row = lax.broadcasted_iota(jnp.int32, shape, 0)
    return halo + row * QUERIES + lax.broadcasted_iota(jnp.int32, shape, 1)


def rows_of(block):
    return pl.ds(pl.multiple_of(block * BLOCK, BLOCK), BLOCK)


def by_reach(count, body):
    for n in range(2, REACH + 1):
        pl.when(count == n)(functools.partial(body, n))


def late(j, n):
    return slice(BLOCK, QUERIES) if j == n - 1 else slice(0, QUERIES)


def valid_of(key_iota, causal, bound, j, n):
    span = late(j, n)
    valid = key_iota[:, span] >= bound[:, span] - j * BLOCK
    if j == n - 1:
        return valid & causal[:, :BLOCK]
    return valid & causal if j == n - 2 else valid


def fold(parts, combine, reduce):
    if reduce is not None:
        parts = [reduce(p.reshape(p.shape[0] // 8, 8, p.shape[1]), axis=0) for p in parts]
    whole = functools.reduce(combine, parts[:-1])
    return jnp.concatenate([whole[:, :BLOCK], combine(whole[:, BLOCK:], parts[-1])], axis=1)


def forward_kernel(
    halo, index_ref, message_ref, own_ref, other_ref, seg_ref, readout_ref,
    total_ref, reward_ref, starts_ref,
    key_s, side_s, bound_s,
):
    heads, tokens = message_ref.shape[0], message_ref.shape[0] * 128
    key_blocks = own_ref.shape[0]
    shift = halo // BLOCK
    index = index_ref[0]
    head = lax.rem(index, heads)
    even = lax.rem(index, 2) == 0
    low_bits = jnp.bfloat16

    weights = jnp.broadcast_to(readout_ref[pl.ds(head, 1), :], (8, 128))
    part = lax.broadcasted_iota(jnp.int32, (8, 128), 0)
    high = weights.astype(low_bits).astype(jnp.float32)
    middle = (weights - high).astype(low_bits).astype(jnp.float32)
    rest = weights - high - middle
    split = jnp.where(part == 0, high, jnp.where(part == 1, middle, rest))
    split = jnp.where(part < 3, split, 0.0).astype(low_bits)
    side = lax.broadcasted_iota(jnp.int32, (8, 128), 0)

    def place(keys, values):
        for s in range(key_blocks):
            key_s[s * 128 : (s + 1) * 128, :] = keys[s]
            worth = jnp.sum(dot(split, values[s], NT), axis=0, keepdims=True)
            worth_high = worth.astype(low_bits).astype(jnp.float32)
            lines = jnp.where(side == 0, worth_high, jnp.where(side == 1, worth - worth_high, 0.0))
            side_s[:, s * 128 : (s + 1) * 128] = jnp.where(side == 2, 1.0, lines).astype(low_bits)

    @pl.when(even)
    def _():
        place(own_ref, other_ref)

    @pl.when(jnp.logical_not(even))
    def _():
        place(other_ref, own_ref)

    starts = starts_of(seg_ref[...])
    for n, start in enumerate(starts):
        starts_ref[n] = start
    bound_s[...] = begin_of(starts, tokens_of(tokens, halo))
    key_iota = lax.broadcasted_iota(jnp.int32, (BLOCK, QUERIES), 0)
    query_iota = lax.broadcasted_iota(jnp.int32, (BLOCK, QUERIES), 1)
    causal = key_iota <= query_iota

    def query_block(i, _):
        first = lax.div(begin_of(starts, halo + i * QUERIES), BLOCK)

        def body(n):
            query = message_ref[pl.ds(4 * i, 4), 0:128, :].reshape(QUERIES, 128)
            bound = bound_s[pl.ds(i, 1), :] - first * BLOCK
            scores = []
            for j in range(n):
                span = late(j, n)
                score = dot(key_s[rows_of(first + j), :], query[span], NT)
                scores.append(jnp.where(valid_of(key_iota, causal, bound, j, n), score, NEGATIVE))
            top = jnp.max(fold(scores, jnp.maximum, jnp.max), axis=0, keepdims=True)
            sums = []
            for j in range(n):
                prob = jnp.exp2((scores[j] - top[:, late(j, n)]) * (SCALE * LOG2E))
                sums.append(dot(side_s[:, rows_of(first + j)], prob.astype(low_bits), NN))
            sums = fold(sums, jnp.add, None)
            reward = (sums[0:1] + sums[1:2]) / sums[2:3]
            total_ref[pl.ds(i, 1), :] = top * (SCALE * LOG2E) + jnp.log2(sums[2:3])
            for part in range(4):
                reward_ref[pl.ds(4 * i + part, 1), :] = reward[:, part * 128 : (part + 1) * 128]

        by_reach(2 * i + 2 + shift - first, body)
        return 0

    lax.fori_loop(0, tokens // QUERIES, query_block, 0)


def backward_kernel(
    halo, index_ref, starts_ref, message_ref, own_ref, other_ref, grad_ref, readout_ref, reward_ref,
    flag_ref, total_ref,
    query_ref, keep_ref, send_ref,
    key_s, turned_s, value_s, grad_s, bound_s, key_grad_s, value_grad_s,
):
    heads, tokens = message_ref.shape[0], message_ref.shape[0] * 128
    key_blocks = own_ref.shape[0]
    shift = halo // BLOCK
    index = index_ref[0]
    head = lax.rem(index, heads)
    even = lax.rem(index, 2) == 0

    def place(keys, values):
        for s in range(key_blocks):
            key_s[s * 128 : (s + 1) * 128, :] = keys[s]
            turned_s[:, s * 128 : (s + 1) * 128] = keys[s].T
            value_s[s * 128 : (s + 1) * 128, :] = values[s]

    @pl.when(even)
    def _():
        place(own_ref, other_ref)

    @pl.when(jnp.logical_not(even))
    def _():
        place(other_ref, own_ref)

    live = flag_ref[0]
    probe = live * (jax.nn.sigmoid(reward_ref[...]) - flag_ref[1])
    live_t, probe_t = live.T, probe.T
    weights = readout_ref[pl.ds(head, 1), :]
    for s in range(heads):
        grad = live_t[:, s : s + 1] * grad_ref[s].astype(jnp.float32)
        grad_s[s] = (grad + probe_t[:, s : s + 1] * weights).astype(jnp.bfloat16)

    starts = [starts_ref[n] for n in range(4)]
    bound_s[...] = begin_of(starts, tokens_of(tokens, halo))
    key_iota = lax.broadcasted_iota(jnp.int32, (BLOCK, QUERIES), 0)
    query_iota = lax.broadcasted_iota(jnp.int32, (BLOCK, QUERIES), 1)
    causal = key_iota <= query_iota
    if halo:
        key_grad_s[:halo, :] = jnp.zeros((halo, 128), jnp.float32)
        value_grad_s[:halo, :] = jnp.zeros((halo, 128), jnp.float32)

    def query_block(i, _):
        first = lax.div(begin_of(starts, halo + i * QUERIES), BLOCK)

        def body(n):
            grad = grad_s[pl.ds(4 * i, 4)].reshape(QUERIES, 128)
            query = message_ref[pl.ds(4 * i, 4), 0:128, :].reshape(QUERIES, 128)
            bound = bound_s[pl.ds(i, 1), :] - first * BLOCK
            total = total_ref[pl.ds(i, 1), :]
            probs, grad_probs, deltas = [], [], []
            for j in range(n):
                rows, span = rows_of(first + j), late(j, n)
                score = dot(key_s[rows, :], query[span], NT) * (SCALE * LOG2E) - total[:, span]
                valid = valid_of(key_iota, causal, bound, j, n)
                prob = jnp.exp2(jnp.where(valid, score, NEGATIVE))
                grad_prob = dot(value_s[rows, :], grad[span], NT)
                deltas.append(prob * grad_prob)
                value_grad = dot(prob.astype(jnp.bfloat16), grad[span], NN)
                if j >= n - 2:
                    value_grad_s[rows, :] = value_grad
                else:
                    value_grad_s[rows, :] += value_grad
                probs.append(prob)
                grad_probs.append(grad_prob)
            delta = jnp.sum(fold(deltas, jnp.add, jnp.sum), axis=0, keepdims=True)
            query_grads = []
            for j in range(n):
                rows, span = rows_of(first + j), late(j, n)
                grad_score = (probs[j] * (grad_probs[j] - delta[:, span])).astype(jnp.bfloat16)
                key_grad = dot(grad_score, query[span], NN)
                if j >= n - 2:
                    key_grad_s[rows, :] = key_grad
                else:
                    key_grad_s[rows, :] += key_grad
                query_grads.append(dot(turned_s[:, rows], grad_score, NN))
            query_grad = (fold(query_grads, jnp.add, None) * SCALE).T.astype(jnp.bfloat16)
            query_ref[pl.ds(4 * i, 4)] = query_grad.reshape(4, 128, 128)

        by_reach(2 * i + 2 + shift - first, body)
        return 0

    lax.fori_loop(0, tokens // QUERIES, query_block, 0)
    shape = keep_ref.shape

    @pl.when(even)
    def _():
        keep_ref[...] = (key_grad_s[...] * SCALE).astype(jnp.bfloat16).reshape(shape)
        send_ref[...] = value_grad_s[...].astype(jnp.bfloat16).reshape(shape)

    @pl.when(jnp.logical_not(even))
    def _():
        keep_ref[...] = value_grad_s[...].astype(jnp.bfloat16).reshape(shape)
        send_ref[...] = (key_grad_s[...] * SCALE).astype(jnp.bfloat16).reshape(shape)


def attention_forward(halo, where, message, own, other, seg, readout):
    heads, depth = message.shape[0], message.shape[2]
    key_tokens = own.shape[0] * own.shape[1]
    count = message.shape[0] * 128 // QUERIES
    return pl.pallas_call(
        functools.partial(forward_kernel, halo),
        out_shape=(
            jax.ShapeDtypeStruct((count, QUERIES), jnp.float32),
            jax.ShapeDtypeStruct((heads, own.shape[1]), jnp.float32),
            jax.ShapeDtypeStruct((4,), jnp.int32),
        ),
        in_specs=[SMEM] + [VMEM] * 5,
        out_specs=(VMEM, VMEM, SMEM),
        scratch_shapes=[
            pltpu.VMEM((key_tokens, depth), jnp.bfloat16),
            pltpu.VMEM((8, key_tokens), jnp.bfloat16),
            pltpu.VMEM((count, QUERIES), jnp.int32),
        ],
        compiler_params=pltpu.CompilerParams(vmem_limit_bytes=24 << 20),
        cost_estimate=pl.CostEstimate(
            flops=4 * BLOCK * QUERIES * depth * count * REACH,
            bytes_accessed=16 << 20,
            transcendentals=BLOCK * QUERIES * count * REACH,
        ),
        name="attention_forward",
    )(where, message, own, other, seg, readout)


def attention_backward(halo, where, starts, message, own, other, grad, readout, reward, flag, total):
    heads, depth = message.shape[0], message.shape[2]
    key_tokens = own.shape[0] * own.shape[1]
    count = message.shape[0] * 128 // QUERIES
    return pl.pallas_call(
        functools.partial(backward_kernel, halo),
        out_shape=(
            jax.ShapeDtypeStruct(grad.shape, jnp.bfloat16),
            jax.ShapeDtypeStruct(own.shape, jnp.bfloat16),
            jax.ShapeDtypeStruct(own.shape, jnp.bfloat16),
        ),
        in_specs=[SMEM, SMEM] + [VMEM] * 8,
        out_specs=(VMEM, VMEM, VMEM),
        scratch_shapes=[
            pltpu.VMEM((key_tokens, depth), jnp.bfloat16),
            pltpu.VMEM((depth, key_tokens), jnp.bfloat16),
            pltpu.VMEM((key_tokens, depth), jnp.bfloat16),
            pltpu.VMEM(grad.shape, jnp.bfloat16),
            pltpu.VMEM((count, QUERIES), jnp.int32),
            pltpu.VMEM((key_tokens, depth), jnp.float32),
            pltpu.VMEM((key_tokens, depth), jnp.float32),
        ],
        compiler_params=pltpu.CompilerParams(vmem_limit_bytes=24 << 20),
        cost_estimate=pl.CostEstimate(
            flops=10 * BLOCK * QUERIES * depth * count * REACH,
            bytes_accessed=16 << 20,
            transcendentals=0,
        ),
        name="attention_backward",
    )(where, starts, message, own, other, grad, readout, reward, flag, total)


def pack_kernel(
    segments_ref, mask_ref, labels_ref, queries_ref, keys_ref, values_ref,
    message_ref, query_s, key_s, value_s, message_s, in_sems, out_sems,
):
    rows, kv_heads = keys_ref.shape[:2]
    copies = [
        pltpu.make_async_copy(source, target, in_sems.at[n])
        for n, (source, target) in enumerate(
            [(queries_ref, query_s), (keys_ref, key_s), (values_ref, value_s)]
        )
    ]
    for copy in copies:
        copy.start()
    line = lax.broadcasted_iota(jnp.int32, (AUX, rows), 0)
    flags = jnp.where(line == 1, mask_ref[...].reshape(1, rows), labels_ref[...].reshape(1, rows))
    flags = jnp.where(line == 0, segments_ref[...].reshape(1, rows), flags)
    flags = flags.astype(jnp.float32).astype(jnp.bfloat16)
    for h in range(2 * kv_heads):
        message_s[h, 2 * rows :, :] = flags

    def send(n, first, last):
        part = (slice(None), slice(first, last))
        return pltpu.make_async_copy(message_s.at[part], message_ref.at[part], out_sems.at[n])

    copies[0].wait()
    message_s[:, :rows, :] = jnp.swapaxes(query_s[...], 0, 1)
    first = send(0, 0, rows)
    first.start()
    copies[1].wait()
    keys = jnp.swapaxes(key_s[...], 0, 1)
    copies[2].wait()
    values = jnp.swapaxes(value_s[...], 0, 1)
    for h in range(kv_heads):
        message_s[2 * h, rows : 2 * rows, :] = keys[h]
        message_s[2 * h + 1, rows : 2 * rows, :] = values[h]
    second = send(1, rows, 2 * rows + AUX)
    second.start()
    first.wait()
    second.wait()


def pack(segments, loss_mask, labels, queries, keys, values):
    rows, heads, depth = queries.shape
    shape = (heads, 2 * rows + AUX, depth)
    return pl.pallas_call(
        pack_kernel,
        out_shape=jax.ShapeDtypeStruct(shape, jnp.bfloat16),
        in_specs=[VMEM] * 3 + [ANY] * 3,
        out_specs=ANY,
        scratch_shapes=[
            pltpu.VMEM(queries.shape, jnp.bfloat16),
            pltpu.VMEM(keys.shape, jnp.bfloat16),
            pltpu.VMEM(values.shape, jnp.bfloat16),
            pltpu.VMEM(shape, jnp.bfloat16),
            pltpu.SemaphoreType.DMA((3,)),
            pltpu.SemaphoreType.DMA((2,)),
        ],
        compiler_params=pltpu.CompilerParams(vmem_limit_bytes=60 << 20),
        name="pack",
    )(segments, loss_mask, labels, queries, keys, values)


def unpack_kernel(home_ref, query_ref, key_ref, value_ref):
    rows = query_ref.shape[0]
    heads = home_ref.shape[0]
    query_ref[...] = jnp.swapaxes(home_ref[:, :rows, :], 0, 1)
    for parity, target in enumerate((key_ref, value_ref)):
        parts = [home_ref[h : h + 1, rows:, :] for h in range(parity, heads, 2)]
        target[...] = jnp.swapaxes(jnp.concatenate(parts, axis=0), 0, 1)


def unpack(home, queries, keys, values):
    return pl.pallas_call(
        unpack_kernel,
        out_shape=tuple(jax.ShapeDtypeStruct(a.shape, a.dtype) for a in (queries, keys, values)),
        in_specs=[VMEM],
        out_specs=(VMEM,) * 3,
        compiler_params=pltpu.CompilerParams(vmem_limit_bytes=24 << 20),
        name="unpack",
    )(home)


def local(queries, keys, values, grad_out, readout, segments, loss_mask, labels):
    rows, heads, depth = queries.shape
    devices = lax.axis_size("context")
    index = lax.axis_index("context")
    clusters = [list(range(s, s + heads)) for s in range(0, devices, heads)]
    many = len(clusters) > 1
    halo = WINDOW if many else 0
    pairs = [(i, i ^ 1) for i in range(devices)]
    bf16, f32 = jnp.bfloat16, jnp.float32

    def exchange(array):
        return lax.all_to_all(
            array, "context", 0, 0, tiled=True, axis_index_groups=clusters if many else None
        )

    def swap(array):
        return lax.ppermute(array, "context", pairs)

    message = pack(segments, loss_mask, labels, queries, keys, values)
    message = exchange(message)
    later, message = lax.optimization_barrier((jnp.transpose(grad_out, (1, 0, 2)), message))
    grad = exchange(later)
    own = message[:, rows : 2 * rows]
    other = swap(own)
    flags = message[:, 2 * rows :]
    seg = flags[:, 0].astype(jnp.int32)
    flag = jnp.stack([flags[:, 1], flags[:, 2]]).astype(f32)
    if many:
        ahead = [(i, i + heads) for i in range(devices - heads)]
        blocks = halo // rows
        far = lax.ppermute((own[-blocks:], other[-blocks:], flags[-blocks:, 0]), "context", ahead)
        own = jnp.concatenate([far[0], own], axis=0)
        other = jnp.concatenate([far[1], other], axis=0)
        far_seg = jnp.where(index < heads, -1, far[2].astype(jnp.int32))
        seg = jnp.concatenate([far_seg, seg], axis=0)

    where = jnp.reshape(index, (1,)).astype(jnp.int32)
    total, reward, starts = attention_forward(halo, where, message, own, other, seg, readout)

    for step in (1, 2, 4, 8):
        reward = reward + lax.ppermute(reward, "context", [(i, i ^ step) for i in range(devices)])

    query_grad, keep, send = attention_backward(
        halo, where, starts, message, own, other, grad, readout, reward, flag, total
    )
    total = keep.astype(f32) + swap(send).astype(f32)
    if many:
        behind = [(i + heads, i) for i in range(devices - heads)]
        back = lax.ppermute(total[:blocks].astype(bf16), "context", behind)
        total = total[blocks:]
        total = total + jnp.pad(
            back.astype(f32), ((heads - blocks, 0), (0, 0), (0, 0))
        )
    home = exchange(jnp.concatenate([query_grad, total.astype(bf16)], axis=1))
    return unpack(home, queries, keys, values)


def solution(mesh):
    sharded = P(("groups", "context"))
    return jax.shard_map(
        local,
        mesh=mesh,
        in_specs=(sharded,) * 4 + (P(),) + (sharded,) * 3,
        out_specs=(sharded,) * 3,
        check_vma=False,
    )
```

```python
import functools
import math

import jax
import jax.numpy as jnp
from jax import lax
from jax.experimental import pallas as pl
from jax.experimental.pallas import tpu as pltpu
from jax.sharding import PartitionSpec as P

WINDOW = 1024
SCALE = 168.0 ** (-0.5)
LOG2E = math.log2(math.e)
NEGATIVE = -1e30
BLOCK = 256
AUX = 8
SEGMENT, MASK, LABEL = 3, 4, 5
QUERIES = 2 * BLOCK
REACH = (WINDOW + QUERIES) // BLOCK
VMEM = pl.BlockSpec(memory_space=pltpu.VMEM)
ANY = pl.BlockSpec(memory_space=pl.ANY)
SMEM = pl.BlockSpec(memory_space=pltpu.SMEM)
NT = (((1,), (1,)), ((), ()))
NN = (((1,), (0,)), ((), ()))


def dot(a, b, dims):
    return lax.dot_general(a, b, dims, preferred_element_type=jnp.float32)


def starts_of(seg_all):
    return [jnp.sum(jnp.where(seg_all < s, 1, 0)) for s in range(4)]


def begin_of(starts, token):
    begin = token - (WINDOW - 1)
    for start in starts:
        begin = jnp.maximum(begin, jnp.where(start <= token, start, 0))
    return begin


def tokens_of(tokens, halo):
    shape = (tokens // QUERIES, QUERIES)
    row = lax.broadcasted_iota(jnp.int32, shape, 0)
    return halo + row * QUERIES + lax.broadcasted_iota(jnp.int32, shape, 1)


def rows_of(block):
    return pl.ds(pl.multiple_of(block * BLOCK, BLOCK), BLOCK)


def by_reach(count, body):
    for n in range(2, REACH + 1):
        pl.when(count == n)(functools.partial(body, n))


def late(j, n):
    return slice(BLOCK, QUERIES) if j == n - 1 else slice(0, QUERIES)


def valid_of(key_iota, causal, bound, j, n):
    span = late(j, n)
    valid = key_iota[:, span] >= bound[:, span] - j * BLOCK
    if j == n - 1:
        return valid & causal[:, :BLOCK]
    return valid & causal if j == n - 2 else valid


def fold(parts, combine, reduce):
    if reduce is not None:
        parts = [reduce(p.reshape(p.shape[0] // 8, 8, p.shape[1]), axis=0) for p in parts]
    whole = functools.reduce(combine, parts[:-1])
    return jnp.concatenate([whole[:, :BLOCK], combine(whole[:, BLOCK:], parts[-1])], axis=1)


def place(even, own_ref, other_ref, put):
    def both(first, second):
        for n in range(first.shape[0]):
            put(n, jnp.concatenate([first[n], second[n]], axis=0))

    pl.when(even)(lambda: both(own_ref, other_ref))
    pl.when(jnp.logical_not(even))(lambda: both(other_ref, own_ref))


def forward_kernel(
    halo, index_ref, message_ref, own_ref, other_ref, seg_ref, lines_ref,
    total_ref, reward_ref, starts_ref,
    key_s, side_s, bound_s,
):
    tokens = message_ref.shape[0] * 128
    shift = halo // BLOCK
    even = lax.rem(index_ref[0], 2) == 0
    low_bits = jnp.bfloat16
    for n in range(lines_ref.shape[0]):
        side_s[:, n * 128 : (n + 1) * 128] = lines_ref[n]

    def put(n, keys):
        key_s[n * 128 : (n + 1) * 128, :] = keys

    place(even, own_ref, other_ref, put)
    starts = starts_of(seg_ref[...])
    for n, start in enumerate(starts):
        starts_ref[n] = start
    bound_s[...] = begin_of(starts, tokens_of(tokens, halo))
    key_iota = lax.broadcasted_iota(jnp.int32, (BLOCK, QUERIES), 0)
    query_iota = lax.broadcasted_iota(jnp.int32, (BLOCK, QUERIES), 1)
    causal = key_iota <= query_iota

    def query_block(i, _):
        first = lax.div(begin_of(starts, halo + i * QUERIES), BLOCK)

        def body(n):
            query = message_ref[pl.ds(4 * i, 4), 0:128, :].reshape(QUERIES, 128)
            bound = bound_s[pl.ds(i, 1), :] - first * BLOCK
            scores = []
            for j in range(n):
                span = late(j, n)
                score = dot(key_s[rows_of(first + j), :], query[span], NT)
                scores.append(jnp.where(valid_of(key_iota, causal, bound, j, n), score, NEGATIVE))
            top = jnp.max(fold(scores, jnp.maximum, jnp.max), axis=0, keepdims=True)
            sums = []
            for j in range(n):
                prob = jnp.exp2((scores[j] - top[:, late(j, n)]) * (SCALE * LOG2E))
                sums.append(dot(side_s[:, rows_of(first + j)], prob.astype(low_bits), NN))
            sums = fold(sums, jnp.add, None)
            reward = (sums[0:1] + sums[1:2]) / sums[2:3]
            total_ref[pl.ds(i, 1), :] = top * (SCALE * LOG2E) + jnp.log2(sums[2:3])
            for part in range(4):
                reward_ref[pl.ds(4 * i + part, 1), :] = reward[:, part * 128 : (part + 1) * 128]

        by_reach(2 * i + 2 + shift - first, body)
        return 0

    lax.fori_loop(0, tokens // QUERIES, query_block, 0)


def backward_kernel(
    halo, index_ref, starts_ref, message_ref, own_ref, other_ref, later_ref, own_value_ref,
    other_value_ref, readout_ref, reward_ref, flag_ref, total_ref,
    query_ref, keep_ref, send_ref,
    key_s, turned_s, value_s, grad_s, bound_s, key_grad_s, value_grad_s,
):
    heads, tokens = message_ref.shape[0], message_ref.shape[0] * 128
    shift = halo // BLOCK
    index = index_ref[0]
    head = lax.rem(index, heads)
    even = lax.rem(index, 2) == 0

    def put_key(n, keys):
        key_s[n * 128 : (n + 1) * 128, :] = keys
        turned_s[:, n * 128 : (n + 1) * 128] = keys.T

    def put_value(n, values):
        value_s[n * 128 : (n + 1) * 128, :] = values

    place(even, own_ref, other_ref, put_key)
    place(even, own_value_ref, other_value_ref, put_value)

    live = flag_ref[0]
    probe = live * (jax.nn.sigmoid(reward_ref[...]) - flag_ref[1])
    live_t, probe_t = live.T, probe.T
    weights = readout_ref[pl.ds(head, 1), :]
    for s in range(heads):
        grad = live_t[:, s : s + 1] * later_ref[s, 0:128, :].astype(jnp.float32)
        grad_s[s] = (grad + probe_t[:, s : s + 1] * weights).astype(jnp.bfloat16)

    starts = [starts_ref[n] for n in range(4)]
    bound_s[...] = begin_of(starts, tokens_of(tokens, halo))
    key_iota = lax.broadcasted_iota(jnp.int32, (BLOCK, QUERIES), 0)
    query_iota = lax.broadcasted_iota(jnp.int32, (BLOCK, QUERIES), 1)
    causal = key_iota <= query_iota
    if halo:
        key_grad_s[:halo, :] = jnp.zeros((halo, 128), jnp.float32)
        value_grad_s[:halo, :] = jnp.zeros((halo, 128), jnp.float32)

    def query_block(i, _):
        first = lax.div(begin_of(starts, halo + i * QUERIES), BLOCK)

        def body(n):
            grad = grad_s[pl.ds(4 * i, 4)].reshape(QUERIES, 128)
            query = message_ref[pl.ds(4 * i, 4), 0:128, :].reshape(QUERIES, 128)
            bound = bound_s[pl.ds(i, 1), :] - first * BLOCK
            total = total_ref[pl.ds(i, 1), :]
            probs, grad_probs, deltas = [], [], []
            for j in range(n):
                rows, span = rows_of(first + j), late(j, n)
                score = dot(key_s[rows, :], query[span], NT) * (SCALE * LOG2E) - total[:, span]
                valid = valid_of(key_iota, causal, bound, j, n)
                prob = jnp.exp2(jnp.where(valid, score, NEGATIVE))
                grad_prob = dot(value_s[rows, :], grad[span], NT)
                deltas.append(prob * grad_prob)
                value_grad = dot(prob.astype(jnp.bfloat16), grad[span], NN)
                if j >= n - 2:
                    value_grad_s[rows, :] = value_grad
                else:
                    value_grad_s[rows, :] += value_grad
                probs.append(prob)
                grad_probs.append(grad_prob)
            delta = jnp.sum(fold(deltas, jnp.add, jnp.sum), axis=0, keepdims=True)
            query_grads = []
            for j in range(n):
                rows, span = rows_of(first + j), late(j, n)
                grad_score = (probs[j] * (grad_probs[j] - delta[:, span])).astype(jnp.bfloat16)
                key_grad = dot(grad_score, query[span], NN)
                if j >= n - 2:
                    key_grad_s[rows, :] = key_grad
                else:
                    key_grad_s[rows, :] += key_grad
                query_grads.append(dot(turned_s[:, rows], grad_score, NN))
            query_grad = (fold(query_grads, jnp.add, None) * SCALE).T.astype(jnp.bfloat16)
            query_ref[pl.ds(4 * i, 4)] = query_grad.reshape(4, 128, 128)

        by_reach(2 * i + 2 + shift - first, body)
        return 0

    lax.fori_loop(0, tokens // QUERIES, query_block, 0)
    shape = keep_ref.shape

    @pl.when(even)
    def _():
        keep_ref[...] = (key_grad_s[...] * SCALE).astype(jnp.bfloat16).reshape(shape)
        send_ref[...] = value_grad_s[...].astype(jnp.bfloat16).reshape(shape)

    @pl.when(jnp.logical_not(even))
    def _():
        keep_ref[...] = value_grad_s[...].astype(jnp.bfloat16).reshape(shape)
        send_ref[...] = (key_grad_s[...] * SCALE).astype(jnp.bfloat16).reshape(shape)


def attention_forward(halo, where, message, own, other, seg, lines):
    heads, depth = message.shape[0], message.shape[2]
    key_tokens = own.shape[0] * 128
    count = message.shape[0] * 128 // QUERIES
    return pl.pallas_call(
        functools.partial(forward_kernel, halo),
        out_shape=(
            jax.ShapeDtypeStruct((count, QUERIES), jnp.float32),
            jax.ShapeDtypeStruct((heads, 128), jnp.float32),
            jax.ShapeDtypeStruct((4,), jnp.int32),
        ),
        in_specs=[SMEM] + [VMEM] * 5,
        out_specs=(VMEM, VMEM, SMEM),
        scratch_shapes=[
            pltpu.VMEM((key_tokens, depth), jnp.bfloat16),
            pltpu.VMEM((8, key_tokens), jnp.bfloat16),
            pltpu.VMEM((count, QUERIES), jnp.int32),
        ],
        compiler_params=pltpu.CompilerParams(vmem_limit_bytes=24 << 20),
        cost_estimate=pl.CostEstimate(
            flops=4 * BLOCK * QUERIES * depth * count * REACH,
            bytes_accessed=16 << 20,
            transcendentals=BLOCK * QUERIES * count * REACH,
        ),
        name="attention_forward",
    )(where, message, own, other, seg, lines)


def attention_backward(
    halo, where, starts, message, own, other, later, own_value, other_value, readout, reward, flag, total
):
    heads, depth = message.shape[0], message.shape[2]
    key_tokens = own.shape[0] * 128
    count = message.shape[0] * 128 // QUERIES
    return pl.pallas_call(
        functools.partial(backward_kernel, halo),
        out_shape=(
            jax.ShapeDtypeStruct((heads, 128, depth), jnp.bfloat16),
            jax.ShapeDtypeStruct((own.shape[0], 128, depth), jnp.bfloat16),
            jax.ShapeDtypeStruct((own.shape[0], 128, depth), jnp.bfloat16),
        ),
        in_specs=[SMEM, SMEM] + [VMEM] * 10,
        out_specs=(VMEM, VMEM, VMEM),
        scratch_shapes=[
            pltpu.VMEM((key_tokens, depth), jnp.bfloat16),
            pltpu.VMEM((depth, key_tokens), jnp.bfloat16),
            pltpu.VMEM((key_tokens, depth), jnp.bfloat16),
            pltpu.VMEM((heads, 128, depth), jnp.bfloat16),
            pltpu.VMEM((count, QUERIES), jnp.int32),
            pltpu.VMEM((key_tokens, depth), jnp.float32),
            pltpu.VMEM((key_tokens, depth), jnp.float32),
        ],
        compiler_params=pltpu.CompilerParams(vmem_limit_bytes=24 << 20),
        cost_estimate=pl.CostEstimate(
            flops=10 * BLOCK * QUERIES * depth * count * REACH,
            bytes_accessed=16 << 20,
            transcendentals=0,
        ),
        name="attention_backward",
    )(
        where, starts, message, own, other, later, own_value, other_value,
        readout, reward, flag, total,
    )


def halves_into(target, start, heads):
    half = heads.shape[1] // 2
    for h in range(2 * heads.shape[0]):
        part = h % 2 * half
        target[h, start : start + half, :] = heads[h // 2, part : part + half]


def pack_kernel(
    readout_ref, segments_ref, mask_ref, labels_ref, queries_ref, keys_ref, values_ref,
    message_ref, segments_s, mask_s, labels_s, query_s, key_s, value_s, message_s, in_sems, out_sems,
):
    rows, kv_heads = keys_ref.shape[:2]
    pairs = [
        (values_ref, value_s), (keys_ref, key_s), (queries_ref, query_s),
        (segments_ref, segments_s), (mask_ref, mask_s), (labels_ref, labels_s),
    ]
    copies = [
        pltpu.make_async_copy(source, target, in_sems.at[n])
        for n, (source, target) in enumerate(pairs)
    ]
    for copy in copies:
        copy.start()

    def send(n, first, last):
        part = (slice(None), slice(first, last))
        return pltpu.make_async_copy(message_s.at[part], message_ref.at[part], out_sems.at[n])

    readout = readout_ref[...]
    high = readout.astype(jnp.bfloat16).astype(jnp.float32)
    middle = (readout - high).astype(jnp.bfloat16).astype(jnp.float32)
    rest = readout - high - middle
    spare = jnp.zeros((2, readout.shape[1]), jnp.float32)
    copies[0].wait()
    values = jnp.swapaxes(value_s[...], 0, 1)
    worths = []
    for c in range(kv_heads):
        parts = [p[h : h + 1] for h in (2 * c, 2 * c + 1) for p in (high, middle, rest)]
        weights = jnp.concatenate(parts + [spare], axis=0).astype(jnp.bfloat16)
        product = dot(weights, values[c], NT)
        worths += [product[0:1] + product[1:2] + product[2:3]]
        worths += [product[3:4] + product[4:5] + product[5:6]]
    copies[1].wait()
    halves_into(message_s, rows, jnp.swapaxes(key_s[...], 0, 1))
    for copy in copies[3:]:
        copy.wait()
    line = lax.broadcasted_iota(jnp.int32, (AUX, rows), 0)
    flags = jnp.ones((AUX, rows), jnp.float32)
    for n, source in ((SEGMENT, segments_s), (MASK, mask_s), (LABEL, labels_s)):
        flags = jnp.where(line == n, source[...].reshape(1, rows).astype(jnp.float32), flags)
    for h, worth in enumerate(worths):
        worth_high = worth.astype(jnp.bfloat16).astype(jnp.float32)
        lines = jnp.where(line == 0, worth_high, jnp.where(line == 1, worth - worth_high, flags))
        message_s[h, rows + rows // 2 :, :] = lines.astype(jnp.bfloat16)
    first = send(0, rows, rows + rows // 2 + AUX)
    first.start()
    copies[2].wait()
    message_s[:, :rows, :] = jnp.swapaxes(query_s[...], 0, 1)
    second = send(1, 0, rows)
    second.start()
    first.wait()
    second.wait()


def pack(readout, segments, loss_mask, labels, queries, keys, values):
    rows, heads, depth = queries.shape
    shape = (heads, rows + rows // 2 + AUX, depth)
    return pl.pallas_call(
        pack_kernel,
        out_shape=jax.ShapeDtypeStruct(shape, jnp.bfloat16),
        in_specs=[VMEM] + [ANY] * 6,
        out_specs=ANY,
        scratch_shapes=[
            pltpu.VMEM(segments.shape, jnp.int32),
            pltpu.VMEM(segments.shape, jnp.int32),
            pltpu.VMEM(segments.shape, jnp.int32),
            pltpu.VMEM(queries.shape, jnp.bfloat16),
            pltpu.VMEM(keys.shape, jnp.bfloat16),
            pltpu.VMEM(values.shape, jnp.bfloat16),
            pltpu.VMEM(shape, jnp.bfloat16),
            pltpu.SemaphoreType.DMA((6,)),
            pltpu.SemaphoreType.DMA((2,)),
        ],
        compiler_params=pltpu.CompilerParams(vmem_limit_bytes=60 << 20),
        name="pack",
    )(readout, segments, loss_mask, labels, queries, keys, values)


def pack_later_kernel(grad_ref, values_ref, message_ref):
    rows = grad_ref.shape[0]
    message_ref[:, :rows, :] = jnp.swapaxes(grad_ref[...], 0, 1)
    halves_into(message_ref, rows, jnp.swapaxes(values_ref[...], 0, 1))


def pack_later(grad_out, values):
    rows, heads, depth = grad_out.shape
    return pl.pallas_call(
        pack_later_kernel,
        out_shape=jax.ShapeDtypeStruct((heads, rows + rows // 2, depth), jnp.bfloat16),
        in_specs=[VMEM] * 2,
        out_specs=VMEM,
        compiler_params=pltpu.CompilerParams(vmem_limit_bytes=16 << 20),
        cost_estimate=pl.CostEstimate(flops=0, bytes_accessed=3 << 20, transcendentals=0),
        name="pack_later",
    )(grad_out, values)


def unpack_kernel(home_ref, query_ref, key_ref, value_ref):
    rows = query_ref.shape[0]
    heads = home_ref.shape[0]
    query_ref[...] = jnp.swapaxes(home_ref[:, :rows, :], 0, 1)
    for parity, target in enumerate((key_ref, value_ref)):
        parts = [home_ref[h : h + 1, rows:, :] for h in range(parity, heads, 2)]
        target[...] = jnp.swapaxes(jnp.concatenate(parts, axis=0), 0, 1)


def unpack(home, queries, keys, values):
    return pl.pallas_call(
        unpack_kernel,
        out_shape=tuple(jax.ShapeDtypeStruct(a.shape, a.dtype) for a in (queries, keys, values)),
        in_specs=[VMEM],
        out_specs=(VMEM,) * 3,
        compiler_params=pltpu.CompilerParams(vmem_limit_bytes=24 << 20),
        name="unpack",
    )(home)


def local(queries, keys, values, grad_out, readout, segments, loss_mask, labels):
    rows, heads, depth = queries.shape
    devices = lax.axis_size("context")
    index = lax.axis_index("context")
    clusters = [list(range(s, s + heads)) for s in range(0, devices, heads)]
    many = len(clusters) > 1
    halo = WINDOW if many else 0
    pairs = [(i, i ^ 1) for i in range(devices)]
    bf16, f32 = jnp.bfloat16, jnp.float32

    def exchange(array):
        return lax.all_to_all(
            array, "context", 0, 0, tiled=True, axis_index_groups=clusters if many else None
        )

    def swap(array):
        return lax.ppermute(array, "context", pairs)

    def split(array):
        own = array[:, rows : rows + rows // 2]
        return own, swap(own)

    def from_before(array):
        if not many:
            return array
        ahead = [(i, i + heads) for i in range(devices - heads)]
        far = lax.ppermute(array[-blocks:], "context", ahead)
        return jnp.concatenate([far, array], axis=0)

    blocks = halo // rows
    message = exchange(pack(readout, segments, loss_mask, labels, queries, keys, values))
    later, message = lax.optimization_barrier((pack_later(grad_out, values), message))
    later = exchange(later)
    own, other = split(message)
    lines = message[:, rows + rows // 2 :]
    flag = jnp.stack([lines[:, MASK], lines[:, LABEL]]).astype(f32)
    lines, own, other = from_before(lines), from_before(own), from_before(other)
    seg = lines[:, SEGMENT].astype(jnp.int32)
    if many:
        place_of = jnp.arange(blocks + heads, dtype=jnp.int32)[:, None]
        seg = jnp.where((index < heads) & (place_of < blocks), -1, seg)
    where = jnp.reshape(index, (1,)).astype(jnp.int32)
    total, reward, starts = attention_forward(halo, where, message, own, other, seg, lines)

    for step in (1, 2, 4, 8):
        reward = reward + lax.ppermute(reward, "context", [(i, i ^ step) for i in range(devices)])

    later, reward = lax.optimization_barrier((later, reward))
    own_value, other_value = split(later)
    query_grad, keep, send = attention_backward(
        halo, where, starts, message, own, other, later, from_before(own_value),
        from_before(other_value), readout, reward, flag, total,
    )
    total = keep.astype(f32) + swap(send).astype(f32)
    if many:
        behind = [(i + heads, i) for i in range(devices - heads)]
        back = lax.ppermute(total[:blocks].astype(bf16), "context", behind)
        total = total[blocks:]
        total = total + jnp.pad(
            back.astype(f32), ((heads - blocks, 0), (0, 0), (0, 0))
        )
    home = exchange(jnp.concatenate([query_grad, total.astype(bf16)], axis=1))
    return unpack(home, queries, keys, values)


def solution(mesh):
    sharded = P(("groups", "context"))
    return jax.shard_map(
        local,
        mesh=mesh,
        in_specs=(sharded,) * 4 + (P(),) + (sharded,) * 3,
        out_specs=(sharded,) * 3,
        check_vma=False,
    )
```

```python
import functools
import math

import jax
import jax.numpy as jnp
from jax import lax
from jax.experimental import pallas as pl
from jax.experimental.pallas import tpu as pltpu
from jax.sharding import PartitionSpec as P

WINDOW = 1024
SCALE = 168.0 ** (-0.5)
LOG2E = math.log2(math.e)
NEGATIVE = -1e30
BLOCK = 256
AUX = 8
SEGMENT, MASK, LABEL = 3, 4, 5
QUERIES = 2 * BLOCK
REACH = (WINDOW + QUERIES) // BLOCK
VMEM = pl.BlockSpec(memory_space=pltpu.VMEM)
ANY = pl.BlockSpec(memory_space=pl.ANY)
SMEM = pl.BlockSpec(memory_space=pltpu.SMEM)
NT = (((1,), (1,)), ((), ()))
NN = (((1,), (0,)), ((), ()))


def dot(a, b, dims):
    return lax.dot_general(a, b, dims, preferred_element_type=jnp.float32)


def starts_of(seg_all):
    return [jnp.sum(jnp.where(seg_all < s, 1, 0)) for s in range(4)]


def begin_of(starts, token):
    begin = token - (WINDOW - 1)
    for start in starts:
        begin = jnp.maximum(begin, jnp.where(start <= token, start, 0))
    return begin


def tokens_of(tokens, halo):
    shape = (tokens // QUERIES, QUERIES)
    row = lax.broadcasted_iota(jnp.int32, shape, 0)
    return halo + row * QUERIES + lax.broadcasted_iota(jnp.int32, shape, 1)


def rows_of(block):
    return pl.ds(pl.multiple_of(block * BLOCK, BLOCK), BLOCK)


def by_reach(count, body):
    for n in range(2, REACH + 1):
        pl.when(count == n)(functools.partial(body, n))


def late(j, n):
    return slice(BLOCK, QUERIES) if j == n - 1 else slice(0, QUERIES)


def valid_of(key_iota, causal, bound, j, n):
    span = late(j, n)
    valid = key_iota[:, span] >= bound[:, span] - j * BLOCK
    if j == n - 1:
        return valid & causal[:, :BLOCK]
    return valid & causal if j == n - 2 else valid


def fold(parts, combine, reduce):
    if reduce is not None:
        parts = [reduce(p.reshape(p.shape[0] // 8, 8, p.shape[1]), axis=0) for p in parts]
    whole = functools.reduce(combine, parts[:-1])
    return jnp.concatenate([whole[:, :BLOCK], combine(whole[:, BLOCK:], parts[-1])], axis=1)


def place(even, own_ref, other_ref, put):
    def both(first, second):
        for n in range(first.shape[0]):
            put(n, jnp.concatenate([first[n], second[n]], axis=0))

    pl.when(even)(lambda: both(own_ref, other_ref))
    pl.when(jnp.logical_not(even))(lambda: both(other_ref, own_ref))


def forward_kernel(
    halo, index_ref, message_ref, own_ref, other_ref, seg_ref, lines_ref,
    total_ref, reward_ref, starts_ref,
    key_s, side_s, bound_s,
):
    tokens = message_ref.shape[0] * 128
    shift = halo // BLOCK
    even = lax.rem(index_ref[0], 2) == 0
    low_bits = jnp.bfloat16
    for n in range(lines_ref.shape[0]):
        side_s[:, n * 128 : (n + 1) * 128] = lines_ref[n]

    def put(n, keys):
        key_s[n * 128 : (n + 1) * 128, :] = keys

    place(even, own_ref, other_ref, put)
    starts = starts_of(seg_ref[...])
    for n, start in enumerate(starts):
        starts_ref[n] = start
    bound_s[...] = begin_of(starts, tokens_of(tokens, halo))
    key_iota = lax.broadcasted_iota(jnp.int32, (BLOCK, QUERIES), 0)
    query_iota = lax.broadcasted_iota(jnp.int32, (BLOCK, QUERIES), 1)
    causal = key_iota <= query_iota

    def query_block(i, _):
        first = lax.div(begin_of(starts, halo + i * QUERIES), BLOCK)

        def body(n):
            query = message_ref[pl.ds(4 * i, 4), 0:128, :].reshape(QUERIES, 128)
            bound = bound_s[pl.ds(i, 1), :] - first * BLOCK
            scores = []
            for j in range(n):
                span = late(j, n)
                score = dot(key_s[rows_of(first + j), :], query[span], NT)
                scores.append(jnp.where(valid_of(key_iota, causal, bound, j, n), score, NEGATIVE))
            top = jnp.max(fold(scores, jnp.maximum, jnp.max), axis=0, keepdims=True)
            sums = []
            for j in range(n):
                prob = jnp.exp2((scores[j] - top[:, late(j, n)]) * (SCALE * LOG2E))
                sums.append(dot(side_s[:, rows_of(first + j)], prob.astype(low_bits), NN))
            sums = fold(sums, jnp.add, None)
            reward = (sums[0:1] + sums[1:2]) / sums[2:3]
            total_ref[pl.ds(i, 1), :] = top * (SCALE * LOG2E) + jnp.log2(sums[2:3])
            for part in range(4):
                reward_ref[pl.ds(4 * i + part, 1), :] = reward[:, part * 128 : (part + 1) * 128]

        by_reach(2 * i + 2 + shift - first, body)
        return 0

    lax.fori_loop(0, tokens // QUERIES, query_block, 0)


def backward_kernel(
    halo, index_ref, starts_ref, message_ref, own_ref, other_ref, later_ref, own_value_ref,
    other_value_ref, readout_ref, reward_ref, flag_ref, total_ref,
    query_ref, keep_ref, send_ref,
    key_s, turned_s, value_s, grad_s, bound_s, key_grad_s, value_grad_s,
):
    heads, tokens = message_ref.shape[0], message_ref.shape[0] * 128
    shift = halo // BLOCK
    index = index_ref[0]
    head = lax.rem(index, heads)
    even = lax.rem(index, 2) == 0

    def put_key(n, keys):
        key_s[n * 128 : (n + 1) * 128, :] = keys
        turned_s[:, n * 128 : (n + 1) * 128] = keys.T

    def put_value(n, values):
        value_s[n * 128 : (n + 1) * 128, :] = values

    place(even, own_ref, other_ref, put_key)
    place(even, own_value_ref, other_value_ref, put_value)

    live = flag_ref[0]
    probe = live * (jax.nn.sigmoid(reward_ref[...]) - flag_ref[1])
    live_t, probe_t = live.T, probe.T
    weights = readout_ref[pl.ds(head, 1), :]
    for s in range(heads):
        grad = live_t[:, s : s + 1] * later_ref[s, 0:128, :].astype(jnp.float32)
        grad_s[s] = (grad + probe_t[:, s : s + 1] * weights).astype(jnp.bfloat16)

    starts = [starts_ref[n] for n in range(4)]
    bound_s[...] = begin_of(starts, tokens_of(tokens, halo))
    key_iota = lax.broadcasted_iota(jnp.int32, (BLOCK, QUERIES), 0)
    query_iota = lax.broadcasted_iota(jnp.int32, (BLOCK, QUERIES), 1)
    causal = key_iota <= query_iota
    if halo:
        key_grad_s[:halo, :] = jnp.zeros((halo, 128), jnp.float32)
        value_grad_s[:halo, :] = jnp.zeros((halo, 128), jnp.float32)

    def query_block(i, _):
        first = lax.div(begin_of(starts, halo + i * QUERIES), BLOCK)

        def body(n):
            grad = grad_s[pl.ds(4 * i, 4)].reshape(QUERIES, 128)
            query = message_ref[pl.ds(4 * i, 4), 0:128, :].reshape(QUERIES, 128)
            bound = bound_s[pl.ds(i, 1), :] - first * BLOCK
            total = total_ref[pl.ds(i, 1), :]
            probs, grad_probs, deltas = [], [], []
            for j in range(n):
                rows, span = rows_of(first + j), late(j, n)
                score = dot(key_s[rows, :], query[span], NT) * (SCALE * LOG2E) - total[:, span]
                valid = valid_of(key_iota, causal, bound, j, n)
                prob = jnp.exp2(jnp.where(valid, score, NEGATIVE))
                grad_prob = dot(value_s[rows, :], grad[span], NT)
                deltas.append(prob * grad_prob)
                value_grad = dot(prob.astype(jnp.bfloat16), grad[span], NN)
                if j >= n - 2:
                    value_grad_s[rows, :] = value_grad
                else:
                    value_grad_s[rows, :] += value_grad
                probs.append(prob)
                grad_probs.append(grad_prob)
            delta = jnp.sum(fold(deltas, jnp.add, jnp.sum), axis=0, keepdims=True)
            query_grads = []
            for j in range(n):
                rows, span = rows_of(first + j), late(j, n)
                grad_score = (probs[j] * (grad_probs[j] - delta[:, span])).astype(jnp.bfloat16)
                key_grad = dot(grad_score, query[span], NN)
                if j >= n - 2:
                    key_grad_s[rows, :] = key_grad
                else:
                    key_grad_s[rows, :] += key_grad
                query_grads.append(dot(turned_s[:, rows], grad_score, NN))
            query_grad = (fold(query_grads, jnp.add, None) * SCALE).T.astype(jnp.bfloat16)
            query_ref[pl.ds(4 * i, 4)] = query_grad.reshape(4, 128, 128)

        by_reach(2 * i + 2 + shift - first, body)
        return 0

    lax.fori_loop(0, tokens // QUERIES, query_block, 0)
    shape = keep_ref.shape

    @pl.when(even)
    def _():
        keep_ref[...] = (key_grad_s[...] * SCALE).astype(jnp.bfloat16).reshape(shape)
        send_ref[...] = value_grad_s[...].astype(jnp.bfloat16).reshape(shape)

    @pl.when(jnp.logical_not(even))
    def _():
        keep_ref[...] = value_grad_s[...].astype(jnp.bfloat16).reshape(shape)
        send_ref[...] = (key_grad_s[...] * SCALE).astype(jnp.bfloat16).reshape(shape)


def attention_forward(halo, where, message, own, other, seg, lines):
    heads, depth = message.shape[0], message.shape[2]
    key_tokens = own.shape[0] * 128
    count = message.shape[0] * 128 // QUERIES
    return pl.pallas_call(
        functools.partial(forward_kernel, halo),
        out_shape=(
            jax.ShapeDtypeStruct((count, QUERIES), jnp.float32),
            jax.ShapeDtypeStruct((heads, 128), jnp.float32),
            jax.ShapeDtypeStruct((4,), jnp.int32),
        ),
        in_specs=[SMEM] + [VMEM] * 5,
        out_specs=(VMEM, VMEM, SMEM),
        scratch_shapes=[
            pltpu.VMEM((key_tokens, depth), jnp.bfloat16),
            pltpu.VMEM((8, key_tokens), jnp.bfloat16),
            pltpu.VMEM((count, QUERIES), jnp.int32),
        ],
        compiler_params=pltpu.CompilerParams(vmem_limit_bytes=24 << 20),
        cost_estimate=pl.CostEstimate(
            flops=4 * BLOCK * QUERIES * depth * count * REACH,
            bytes_accessed=16 << 20,
            transcendentals=BLOCK * QUERIES * count * REACH,
        ),
        name="attention_forward",
    )(where, message, own, other, seg, lines)


def attention_backward(
    halo, where, starts, message, own, other, later, own_value, other_value, readout, reward, flag, total
):
    heads, depth = message.shape[0], message.shape[2]
    key_tokens = own.shape[0] * 128
    count = message.shape[0] * 128 // QUERIES
    return pl.pallas_call(
        functools.partial(backward_kernel, halo),
        out_shape=(
            jax.ShapeDtypeStruct((heads, 128, depth), jnp.bfloat16),
            jax.ShapeDtypeStruct((own.shape[0], 128, depth), jnp.bfloat16),
            jax.ShapeDtypeStruct((own.shape[0], 128, depth), jnp.bfloat16),
        ),
        in_specs=[SMEM, SMEM] + [VMEM] * 10,
        out_specs=(VMEM, VMEM, VMEM),
        scratch_shapes=[
            pltpu.VMEM((key_tokens, depth), jnp.bfloat16),
            pltpu.VMEM((depth, key_tokens), jnp.bfloat16),
            pltpu.VMEM((key_tokens, depth), jnp.bfloat16),
            pltpu.VMEM((heads, 128, depth), jnp.bfloat16),
            pltpu.VMEM((count, QUERIES), jnp.int32),
            pltpu.VMEM((key_tokens, depth), jnp.float32),
            pltpu.VMEM((key_tokens, depth), jnp.float32),
        ],
        compiler_params=pltpu.CompilerParams(vmem_limit_bytes=24 << 20),
        cost_estimate=pl.CostEstimate(
            flops=10 * BLOCK * QUERIES * depth * count * REACH,
            bytes_accessed=16 << 20,
            transcendentals=0,
        ),
        name="attention_backward",
    )(
        where, starts, message, own, other, later, own_value, other_value,
        readout, reward, flag, total,
    )


def halves_into(target, start, heads):
    half = heads.shape[1] // 2
    for h in range(2 * heads.shape[0]):
        part = h % 2 * half
        target[h, start : start + half, :] = heads[h // 2, part : part + half]


def pack_kernel(
    readout_ref, segments_ref, mask_ref, labels_ref, queries_ref, keys_ref, values_ref,
    message_ref, readout_s, segments_s, mask_s, labels_s, query_s, key_s, value_s, message_s,
    in_sems, out_sems,
):
    rows, kv_heads = keys_ref.shape[:2]
    pairs = [
        (queries_ref, query_s), (values_ref, value_s), (keys_ref, key_s), (readout_ref, readout_s),
        (segments_ref, segments_s), (mask_ref, mask_s), (labels_ref, labels_s),
    ]
    copies = [
        pltpu.make_async_copy(source, target, in_sems.at[n])
        for n, (source, target) in enumerate(pairs)
    ]
    for copy in copies:
        copy.start()

    def send(n, first, last):
        part = (slice(None), slice(first, last))
        return pltpu.make_async_copy(message_s.at[part], message_ref.at[part], out_sems.at[n])

    copies[0].wait()
    message_s[:, :rows, :] = jnp.swapaxes(query_s[...], 0, 1)
    first = send(0, 0, rows)
    first.start()
    copies[2].wait()
    halves_into(message_s, rows, jnp.swapaxes(key_s[...], 0, 1))
    second = send(1, rows, rows + rows // 2)
    second.start()
    for copy in copies[3:]:
        copy.wait()
    readout = readout_s[...]
    high = readout.astype(jnp.bfloat16).astype(jnp.float32)
    middle = (readout - high).astype(jnp.bfloat16).astype(jnp.float32)
    rest = readout - high - middle
    spare = jnp.zeros((2, readout.shape[1]), jnp.float32)
    line = lax.broadcasted_iota(jnp.int32, (AUX, rows), 0)
    flags = jnp.ones((AUX, rows), jnp.float32)
    for n, source in ((SEGMENT, segments_s), (MASK, mask_s), (LABEL, labels_s)):
        flags = jnp.where(line == n, source[...].reshape(1, rows).astype(jnp.float32), flags)
    copies[1].wait()
    values = jnp.swapaxes(value_s[...], 0, 1)
    for c in range(kv_heads):
        parts = [p[h : h + 1] for h in (2 * c, 2 * c + 1) for p in (high, middle, rest)]
        weights = jnp.concatenate(parts + [spare], axis=0).astype(jnp.bfloat16)
        product = dot(weights, values[c], NT)
        for h in range(2):
            worth = product[3 * h : 3 * h + 1] + product[3 * h + 1 : 3 * h + 2]
            worth = worth + product[3 * h + 2 : 3 * h + 3]
            worth_high = worth.astype(jnp.bfloat16).astype(jnp.float32)
            lines = jnp.where(line == 0, worth_high, jnp.where(line == 1, worth - worth_high, flags))
            message_s[2 * c + h, rows + rows // 2 :, :] = lines.astype(jnp.bfloat16)
    third = send(2, rows + rows // 2, rows + rows // 2 + AUX)
    third.start()
    first.wait()
    second.wait()
    third.wait()


def pack(readout, segments, loss_mask, labels, queries, keys, values):
    rows, heads, depth = queries.shape
    shape = (heads, rows + rows // 2 + AUX, depth)
    return pl.pallas_call(
        pack_kernel,
        out_shape=jax.ShapeDtypeStruct(shape, jnp.bfloat16),
        in_specs=[ANY] * 7,
        out_specs=ANY,
        scratch_shapes=[
            pltpu.VMEM(readout.shape, jnp.float32),
            pltpu.VMEM(segments.shape, jnp.int32),
            pltpu.VMEM(segments.shape, jnp.int32),
            pltpu.VMEM(segments.shape, jnp.int32),
            pltpu.VMEM(queries.shape, jnp.bfloat16),
            pltpu.VMEM(keys.shape, jnp.bfloat16),
            pltpu.VMEM(values.shape, jnp.bfloat16),
            pltpu.VMEM(shape, jnp.bfloat16),
            pltpu.SemaphoreType.DMA((7,)),
            pltpu.SemaphoreType.DMA((3,)),
        ],
        compiler_params=pltpu.CompilerParams(vmem_limit_bytes=60 << 20),
        name="pack",
    )(readout, segments, loss_mask, labels, queries, keys, values)


def pack_later_kernel(grad_ref, values_ref, message_ref):
    rows = grad_ref.shape[0]
    message_ref[:, :rows, :] = jnp.swapaxes(grad_ref[...], 0, 1)
    halves_into(message_ref, rows, jnp.swapaxes(values_ref[...], 0, 1))


def pack_later(grad_out, values):
    rows, heads, depth = grad_out.shape
    return pl.pallas_call(
        pack_later_kernel,
        out_shape=jax.ShapeDtypeStruct((heads, rows + rows // 2, depth), jnp.bfloat16),
        in_specs=[VMEM] * 2,
        out_specs=VMEM,
        compiler_params=pltpu.CompilerParams(vmem_limit_bytes=16 << 20),
        cost_estimate=pl.CostEstimate(flops=0, bytes_accessed=3 << 20, transcendentals=0),
        name="pack_later",
    )(grad_out, values)


def unpack_kernel(home_ref, query_ref, key_ref, value_ref):
    rows = query_ref.shape[0]
    heads = home_ref.shape[0]
    query_ref[...] = jnp.swapaxes(home_ref[:, :rows, :], 0, 1)
    for parity, target in enumerate((key_ref, value_ref)):
        parts = [home_ref[h : h + 1, rows:, :] for h in range(parity, heads, 2)]
        target[...] = jnp.swapaxes(jnp.concatenate(parts, axis=0), 0, 1)


def unpack(home, queries, keys, values):
    return pl.pallas_call(
        unpack_kernel,
        out_shape=tuple(jax.ShapeDtypeStruct(a.shape, a.dtype) for a in (queries, keys, values)),
        in_specs=[VMEM],
        out_specs=(VMEM,) * 3,
        compiler_params=pltpu.CompilerParams(vmem_limit_bytes=24 << 20),
        name="unpack",
    )(home)


def local(queries, keys, values, grad_out, readout, segments, loss_mask, labels):
    rows, heads, depth = queries.shape
    devices = lax.axis_size("context")
    index = lax.axis_index("context")
    clusters = [list(range(s, s + heads)) for s in range(0, devices, heads)]
    many = len(clusters) > 1
    halo = WINDOW if many else 0
    pairs = [(i, i ^ 1) for i in range(devices)]
    bf16, f32 = jnp.bfloat16, jnp.float32

    def exchange(array):
        return lax.all_to_all(
            array, "context", 0, 0, tiled=True, axis_index_groups=clusters if many else None
        )

    def swap(array):
        return lax.ppermute(array, "context", pairs)

    def split(array):
        own = array[:, rows : rows + rows // 2]
        return own, swap(own)

    def from_before(array):
        if not many:
            return array
        ahead = [(i, i + heads) for i in range(devices - heads)]
        far = lax.ppermute(array[-blocks:], "context", ahead)
        return jnp.concatenate([far, array], axis=0)

    blocks = halo // rows
    message = exchange(pack(readout, segments, loss_mask, labels, queries, keys, values))
    later, message = lax.optimization_barrier((pack_later(grad_out, values), message))
    later = exchange(later)
    own, other = split(message)
    lines = message[:, rows + rows // 2 :]
    flag = jnp.stack([lines[:, MASK], lines[:, LABEL]]).astype(f32)
    lines, own, other = from_before(lines), from_before(own), from_before(other)
    seg = lines[:, SEGMENT].astype(jnp.int32)
    if many:
        place_of = jnp.arange(blocks + heads, dtype=jnp.int32)[:, None]
        seg = jnp.where((index < heads) & (place_of < blocks), -1, seg)
    where = jnp.reshape(index, (1,)).astype(jnp.int32)
    total, reward, starts = attention_forward(halo, where, message, own, other, seg, lines)

    for step in (1, 2, 4, 8):
        reward = reward + lax.ppermute(reward, "context", [(i, i ^ step) for i in range(devices)])

    later, reward = lax.optimization_barrier((later, reward))
    own_value, other_value = split(later)
    query_grad, keep, send = attention_backward(
        halo, where, starts, message, own, other, later, from_before(own_value),
        from_before(other_value), readout, reward, flag, total,
    )
    total = keep.astype(f32) + swap(send).astype(f32)
    if many:
        behind = [(i + heads, i) for i in range(devices - heads)]
        back = lax.ppermute(total[:blocks].astype(bf16), "context", behind)
        total = total[blocks:]
        total = total + jnp.pad(
            back.astype(f32), ((heads - blocks, 0), (0, 0), (0, 0))
        )
    home = exchange(jnp.concatenate([query_grad, total.astype(bf16)], axis=1))
    return unpack(home, queries, keys, values)


def solution(mesh):
    sharded = P(("groups", "context"))
    return jax.shard_map(
        local,
        mesh=mesh,
        in_specs=(sharded,) * 4 + (P(),) + (sharded,) * 3,
        out_specs=(sharded,) * 3,
        check_vma=False,
    )
```

```python
import functools
import math

import jax
import jax.numpy as jnp
from jax import lax
from jax.experimental import pallas as pl
from jax.experimental.pallas import tpu as pltpu
from jax.sharding import PartitionSpec as P

WINDOW = 1024
SCALE = 168.0 ** (-0.5)
LOG2E = math.log2(math.e)
NEGATIVE = -1e30
BLOCK = 256
AUX = 8
SEGMENT, MASK, LABEL = 3, 4, 5
QUERIES = 2 * BLOCK
REACH = (WINDOW + QUERIES) // BLOCK
VMEM = pl.BlockSpec(memory_space=pltpu.VMEM)
ANY = pl.BlockSpec(memory_space=pl.ANY)
SMEM = pl.BlockSpec(memory_space=pltpu.SMEM)
NT = (((1,), (1,)), ((), ()))
NN = (((1,), (0,)), ((), ()))


def dot(a, b, dims):
    return lax.dot_general(a, b, dims, preferred_element_type=jnp.float32)


def starts_of(seg_all):
    return [jnp.sum(jnp.where(seg_all < s, 1, 0)) for s in range(4)]


def begin_of(starts, token):
    begin = token - (WINDOW - 1)
    for start in starts:
        begin = jnp.maximum(begin, jnp.where(start <= token, start, 0))
    return begin


def tokens_of(tokens, halo):
    shape = (tokens // QUERIES, QUERIES)
    row = lax.broadcasted_iota(jnp.int32, shape, 0)
    return halo + row * QUERIES + lax.broadcasted_iota(jnp.int32, shape, 1)


def rows_of(block):
    return pl.ds(pl.multiple_of(block * BLOCK, BLOCK), BLOCK)


def by_reach(count, body):
    for n in range(2, REACH + 1):
        pl.when(count == n)(functools.partial(body, n))


def late(j, n):
    if j == n - 1:
        return slice(BLOCK, QUERIES)
    return slice(0, BLOCK if j == 0 and n == REACH else QUERIES)


def valid_of(key_iota, causal, bound, j, n):
    span = late(j, n)
    valid = key_iota[:, span] >= bound[:, span] - j * BLOCK
    if j == n - 1:
        return valid & causal[:, :BLOCK]
    return valid & causal if j == n - 2 else valid


def fold(parts, combine, reduce):
    if reduce is not None:
        parts = [reduce(p.reshape(p.shape[0] // 8, 8, p.shape[1]), axis=0) for p in parts]
    whole = functools.reduce(combine, [p for p in parts if p.shape[1] == QUERIES])
    early, later = whole[:, :BLOCK], combine(whole[:, BLOCK:], parts[-1])
    if parts[0].shape[1] == BLOCK:
        early = combine(early, parts[0])
    return jnp.concatenate([early, later], axis=1)


def place(even, own_ref, other_ref, put):
    def both(first, second):
        for n in range(first.shape[0]):
            put(n, jnp.concatenate([first[n], second[n]], axis=0))

    pl.when(even)(lambda: both(own_ref, other_ref))
    pl.when(jnp.logical_not(even))(lambda: both(other_ref, own_ref))


def forward_kernel(
    halo, index_ref, message_ref, own_ref, other_ref, seg_ref, lines_ref,
    total_ref, reward_ref, starts_ref,
    key_s, side_s, bound_s,
):
    tokens = message_ref.shape[0] * 128
    shift = halo // BLOCK
    even = lax.rem(index_ref[0], 2) == 0
    low_bits = jnp.bfloat16
    for n in range(lines_ref.shape[0]):
        side_s[:, n * 128 : (n + 1) * 128] = lines_ref[n]

    def put(n, keys):
        key_s[n * 128 : (n + 1) * 128, :] = keys

    place(even, own_ref, other_ref, put)
    starts = starts_of(seg_ref[...])
    for n, start in enumerate(starts):
        starts_ref[n] = start
    bound_s[...] = begin_of(starts, tokens_of(tokens, halo))
    key_iota = lax.broadcasted_iota(jnp.int32, (BLOCK, QUERIES), 0)
    query_iota = lax.broadcasted_iota(jnp.int32, (BLOCK, QUERIES), 1)
    causal = key_iota <= query_iota

    def query_block(i, _):
        first = lax.div(begin_of(starts, halo + i * QUERIES), BLOCK)

        def body(n):
            query = message_ref[pl.ds(4 * i, 4), 0:128, :].reshape(QUERIES, 128)
            bound = bound_s[pl.ds(i, 1), :] - first * BLOCK
            scores = []
            for j in range(n):
                span = late(j, n)
                score = dot(key_s[rows_of(first + j), :], query[span], NT)
                scores.append(jnp.where(valid_of(key_iota, causal, bound, j, n), score, NEGATIVE))
            top = jnp.max(fold(scores, jnp.maximum, jnp.max), axis=0, keepdims=True)
            sums = []
            for j in range(n):
                prob = jnp.exp2((scores[j] - top[:, late(j, n)]) * (SCALE * LOG2E))
                sums.append(dot(side_s[:, rows_of(first + j)], prob.astype(low_bits), NN))
            sums = fold(sums, jnp.add, None)
            reward = (sums[0:1] + sums[1:2]) / sums[2:3]
            total_ref[pl.ds(i, 1), :] = top * (SCALE * LOG2E) + jnp.log2(sums[2:3])
            for part in range(4):
                reward_ref[pl.ds(4 * i + part, 1), :] = reward[:, part * 128 : (part + 1) * 128]

        by_reach(2 * i + 2 + shift - first, body)
        return 0

    lax.fori_loop(0, tokens // QUERIES, query_block, 0)


def backward_kernel(
    halo, index_ref, starts_ref, message_ref, own_ref, other_ref, later_ref, own_value_ref,
    other_value_ref, readout_ref, reward_ref, flag_ref, total_ref,
    query_ref, keep_ref, send_ref,
    key_s, turned_s, value_s, grad_s, bound_s, key_grad_s, value_grad_s,
):
    heads, tokens = message_ref.shape[0], message_ref.shape[0] * 128
    shift = halo // BLOCK
    index = index_ref[0]
    head = lax.rem(index, heads)
    even = lax.rem(index, 2) == 0

    def put_key(n, keys):
        key_s[n * 128 : (n + 1) * 128, :] = keys
        turned_s[:, n * 128 : (n + 1) * 128] = keys.T

    def put_value(n, values):
        value_s[n * 128 : (n + 1) * 128, :] = values

    place(even, own_ref, other_ref, put_key)
    place(even, own_value_ref, other_value_ref, put_value)

    live = flag_ref[0]
    probe = live * (jax.nn.sigmoid(reward_ref[...]) - flag_ref[1])
    live_t, probe_t = live.T, probe.T
    weights = readout_ref[pl.ds(head, 1), :]
    for s in range(heads):
        grad = live_t[:, s : s + 1] * later_ref[s, 0:128, :].astype(jnp.float32)
        grad_s[s] = (grad + probe_t[:, s : s + 1] * weights).astype(jnp.bfloat16)

    starts = [starts_ref[n] for n in range(4)]
    bound_s[...] = begin_of(starts, tokens_of(tokens, halo))
    key_iota = lax.broadcasted_iota(jnp.int32, (BLOCK, QUERIES), 0)
    query_iota = lax.broadcasted_iota(jnp.int32, (BLOCK, QUERIES), 1)
    causal = key_iota <= query_iota
    if halo:
        key_grad_s[:halo, :] = jnp.zeros((halo, 128), jnp.float32)
        value_grad_s[:halo, :] = jnp.zeros((halo, 128), jnp.float32)

    def query_block(i, _):
        first = lax.div(begin_of(starts, halo + i * QUERIES), BLOCK)

        def body(n):
            grad = grad_s[pl.ds(4 * i, 4)].reshape(QUERIES, 128)
            query = message_ref[pl.ds(4 * i, 4), 0:128, :].reshape(QUERIES, 128)
            bound = bound_s[pl.ds(i, 1), :] - first * BLOCK
            total = total_ref[pl.ds(i, 1), :]
            probs, grad_probs, deltas = [], [], []

            def dots(j):
                rows, span = rows_of(first + j), late(j, n)
                return dot(key_s[rows, :], query[span], NT), dot(value_s[rows, :], grad[span], NT)

            ahead = dots(0)
            for j in range(n):
                rows, span = rows_of(first + j), late(j, n)
                score, grad_prob = ahead
                if j < n - 1:
                    ahead = dots(j + 1)
                score = score * (SCALE * LOG2E) - total[:, span]
                valid = valid_of(key_iota, causal, bound, j, n)
                prob = jnp.exp2(jnp.where(valid, score, NEGATIVE))
                deltas.append(prob * grad_prob)
                value_grad = dot(prob.astype(jnp.bfloat16), grad[span], NN)
                if j >= n - 2:
                    value_grad_s[rows, :] = value_grad
                else:
                    value_grad_s[rows, :] += value_grad
                probs.append(prob)
                grad_probs.append(grad_prob)
            delta = jnp.sum(fold(deltas, jnp.add, jnp.sum), axis=0, keepdims=True)
            query_grads = []
            for j in range(n):
                rows, span = rows_of(first + j), late(j, n)
                grad_score = (probs[j] * (grad_probs[j] - delta[:, span])).astype(jnp.bfloat16)
                key_grad = dot(grad_score, query[span], NN)
                if j >= n - 2:
                    key_grad_s[rows, :] = key_grad
                else:
                    key_grad_s[rows, :] += key_grad
                query_grads.append(dot(turned_s[:, rows], grad_score, NN))
            query_grad = (fold(query_grads, jnp.add, None) * SCALE).T.astype(jnp.bfloat16)
            query_ref[pl.ds(4 * i, 4)] = query_grad.reshape(4, 128, 128)

        by_reach(2 * i + 2 + shift - first, body)
        return 0

    lax.fori_loop(0, tokens // QUERIES, query_block, 0)
    shape = keep_ref.shape

    @pl.when(even)
    def _():
        keep_ref[...] = (key_grad_s[...] * SCALE).astype(jnp.bfloat16).reshape(shape)
        send_ref[...] = value_grad_s[...].astype(jnp.bfloat16).reshape(shape)

    @pl.when(jnp.logical_not(even))
    def _():
        keep_ref[...] = value_grad_s[...].astype(jnp.bfloat16).reshape(shape)
        send_ref[...] = (key_grad_s[...] * SCALE).astype(jnp.bfloat16).reshape(shape)


def attention_forward(halo, where, message, own, other, seg, lines):
    heads, depth = message.shape[0], message.shape[2]
    key_tokens = own.shape[0] * 128
    count = message.shape[0] * 128 // QUERIES
    return pl.pallas_call(
        functools.partial(forward_kernel, halo),
        out_shape=(
            jax.ShapeDtypeStruct((count, QUERIES), jnp.float32),
            jax.ShapeDtypeStruct((heads, 128), jnp.float32),
            jax.ShapeDtypeStruct((4,), jnp.int32),
        ),
        in_specs=[SMEM] + [VMEM] * 5,
        out_specs=(VMEM, VMEM, SMEM),
        scratch_shapes=[
            pltpu.VMEM((key_tokens, depth), jnp.bfloat16),
            pltpu.VMEM((8, key_tokens), jnp.bfloat16),
            pltpu.VMEM((count, QUERIES), jnp.int32),
        ],
        compiler_params=pltpu.CompilerParams(vmem_limit_bytes=24 << 20),
        cost_estimate=pl.CostEstimate(
            flops=4 * BLOCK * QUERIES * depth * count * REACH,
            bytes_accessed=16 << 20,
            transcendentals=BLOCK * QUERIES * count * REACH,
        ),
        name="attention_forward",
    )(where, message, own, other, seg, lines)


def attention_backward(
    halo, where, starts, message, own, other, later, own_value, other_value, readout, reward, flag, total
):
    heads, depth = message.shape[0], message.shape[2]
    key_tokens = own.shape[0] * 128
    count = message.shape[0] * 128 // QUERIES
    return pl.pallas_call(
        functools.partial(backward_kernel, halo),
        out_shape=(
            jax.ShapeDtypeStruct((heads, 128, depth), jnp.bfloat16),
            jax.ShapeDtypeStruct((own.shape[0], 128, depth), jnp.bfloat16),
            jax.ShapeDtypeStruct((own.shape[0], 128, depth), jnp.bfloat16),
        ),
        in_specs=[SMEM, SMEM] + [VMEM] * 10,
        out_specs=(VMEM, VMEM, VMEM),
        scratch_shapes=[
            pltpu.VMEM((key_tokens, depth), jnp.bfloat16),
            pltpu.VMEM((depth, key_tokens), jnp.bfloat16),
            pltpu.VMEM((key_tokens, depth), jnp.bfloat16),
            pltpu.VMEM((heads, 128, depth), jnp.bfloat16),
            pltpu.VMEM((count, QUERIES), jnp.int32),
            pltpu.VMEM((key_tokens, depth), jnp.float32),
            pltpu.VMEM((key_tokens, depth), jnp.float32),
        ],
        compiler_params=pltpu.CompilerParams(vmem_limit_bytes=24 << 20),
        cost_estimate=pl.CostEstimate(
            flops=10 * BLOCK * QUERIES * depth * count * REACH,
            bytes_accessed=16 << 20,
            transcendentals=0,
        ),
        name="attention_backward",
    )(
        where, starts, message, own, other, later, own_value, other_value,
        readout, reward, flag, total,
    )


def halves_into(target, start, heads):
    half = heads.shape[1] // 2
    for h in range(2 * heads.shape[0]):
        part = h % 2 * half
        target[h, start : start + half, :] = heads[h // 2, part : part + half]


def pack_kernel(
    readout_ref, segments_ref, mask_ref, labels_ref, queries_ref, keys_ref, values_ref,
    message_ref, readout_s, segments_s, mask_s, labels_s, query_s, key_s, value_s, message_s,
    in_sems, out_sems,
):
    rows, kv_heads = keys_ref.shape[:2]
    pairs = [
        (queries_ref, query_s), (values_ref, value_s), (keys_ref, key_s), (readout_ref, readout_s),
        (segments_ref, segments_s), (mask_ref, mask_s), (labels_ref, labels_s),
    ]
    copies = [
        pltpu.make_async_copy(source, target, in_sems.at[n])
        for n, (source, target) in enumerate(pairs)
    ]
    for copy in copies:
        copy.start()

    def send(n, first, last):
        part = (slice(None), slice(first, last))
        return pltpu.make_async_copy(message_s.at[part], message_ref.at[part], out_sems.at[n])

    copies[0].wait()
    message_s[:, :rows, :] = jnp.swapaxes(query_s[...], 0, 1)
    first = send(0, 0, rows)
    first.start()
    copies[2].wait()
    halves_into(message_s, rows, jnp.swapaxes(key_s[...], 0, 1))
    second = send(1, rows, rows + rows // 2)
    second.start()
    for copy in copies[3:]:
        copy.wait()
    readout = readout_s[...]
    high = readout.astype(jnp.bfloat16).astype(jnp.float32)
    middle = (readout - high).astype(jnp.bfloat16).astype(jnp.float32)
    rest = readout - high - middle
    spare = jnp.zeros((2, readout.shape[1]), jnp.float32)
    line = lax.broadcasted_iota(jnp.int32, (AUX, rows), 0)
    flags = jnp.ones((AUX, rows), jnp.float32)
    for n, source in ((SEGMENT, segments_s), (MASK, mask_s), (LABEL, labels_s)):
        flags = jnp.where(line == n, source[...].reshape(1, rows).astype(jnp.float32), flags)
    copies[1].wait()
    values = jnp.swapaxes(value_s[...], 0, 1)
    for c in range(kv_heads):
        parts = [p[h : h + 1] for h in (2 * c, 2 * c + 1) for p in (high, middle, rest)]
        weights = jnp.concatenate(parts + [spare], axis=0).astype(jnp.bfloat16)
        product = dot(weights, values[c], NT)
        for h in range(2):
            worth = product[3 * h : 3 * h + 1] + product[3 * h + 1 : 3 * h + 2]
            worth = worth + product[3 * h + 2 : 3 * h + 3]
            worth_high = worth.astype(jnp.bfloat16).astype(jnp.float32)
            lines = jnp.where(line == 0, worth_high, jnp.where(line == 1, worth - worth_high, flags))
            message_s[2 * c + h, rows + rows // 2 :, :] = lines.astype(jnp.bfloat16)
    third = send(2, rows + rows // 2, rows + rows // 2 + AUX)
    third.start()
    first.wait()
    second.wait()
    third.wait()


def pack(readout, segments, loss_mask, labels, queries, keys, values):
    rows, heads, depth = queries.shape
    shape = (heads, rows + rows // 2 + AUX, depth)
    return pl.pallas_call(
        pack_kernel,
        out_shape=jax.ShapeDtypeStruct(shape, jnp.bfloat16),
        in_specs=[ANY] * 7,
        out_specs=ANY,
        scratch_shapes=[
            pltpu.VMEM(readout.shape, jnp.float32),
            pltpu.VMEM(segments.shape, jnp.int32),
            pltpu.VMEM(segments.shape, jnp.int32),
            pltpu.VMEM(segments.shape, jnp.int32),
            pltpu.VMEM(queries.shape, jnp.bfloat16),
            pltpu.VMEM(keys.shape, jnp.bfloat16),
            pltpu.VMEM(values.shape, jnp.bfloat16),
            pltpu.VMEM(shape, jnp.bfloat16),
            pltpu.SemaphoreType.DMA((7,)),
            pltpu.SemaphoreType.DMA((3,)),
        ],
        compiler_params=pltpu.CompilerParams(vmem_limit_bytes=60 << 20),
        name="pack",
    )(readout, segments, loss_mask, labels, queries, keys, values)


def pack_later_kernel(grad_ref, values_ref, message_ref):
    rows = grad_ref.shape[0]
    message_ref[:, :rows, :] = jnp.swapaxes(grad_ref[...], 0, 1)
    halves_into(message_ref, rows, jnp.swapaxes(values_ref[...], 0, 1))


def pack_later(grad_out, values):
    rows, heads, depth = grad_out.shape
    return pl.pallas_call(
        pack_later_kernel,
        out_shape=jax.ShapeDtypeStruct((heads, rows + rows // 2, depth), jnp.bfloat16),
        in_specs=[VMEM] * 2,
        out_specs=VMEM,
        compiler_params=pltpu.CompilerParams(vmem_limit_bytes=16 << 20),
        cost_estimate=pl.CostEstimate(flops=0, bytes_accessed=3 << 20, transcendentals=0),
        name="pack_later",
    )(grad_out, values)


def unpack_kernel(home_ref, query_ref, key_ref, value_ref):
    rows = query_ref.shape[0]
    heads = home_ref.shape[0]
    query_ref[...] = jnp.swapaxes(home_ref[:, :rows, :], 0, 1)
    for parity, target in enumerate((key_ref, value_ref)):
        parts = [home_ref[h : h + 1, rows:, :] for h in range(parity, heads, 2)]
        target[...] = jnp.swapaxes(jnp.concatenate(parts, axis=0), 0, 1)


def unpack(home, queries, keys, values):
    return pl.pallas_call(
        unpack_kernel,
        out_shape=tuple(jax.ShapeDtypeStruct(a.shape, a.dtype) for a in (queries, keys, values)),
        in_specs=[VMEM],
        out_specs=(VMEM,) * 3,
        compiler_params=pltpu.CompilerParams(vmem_limit_bytes=24 << 20),
        name="unpack",
    )(home)


def local(queries, keys, values, grad_out, readout, segments, loss_mask, labels):
    rows, heads, depth = queries.shape
    devices = lax.axis_size("context")
    index = lax.axis_index("context")
    clusters = [list(range(s, s + heads)) for s in range(0, devices, heads)]
    many = len(clusters) > 1
    halo = WINDOW if many else 0
    pairs = [(i, i ^ 1) for i in range(devices)]
    bf16, f32 = jnp.bfloat16, jnp.float32

    def exchange(array):
        return lax.all_to_all(
            array, "context", 0, 0, tiled=True, axis_index_groups=clusters if many else None
        )

    def swap(array):
        return lax.ppermute(array, "context", pairs)

    def split(array):
        own = array[:, rows : rows + rows // 2]
        return own, swap(own)

    def from_before(array):
        if not many:
            return array
        ahead = [(i, i + heads) for i in range(devices - heads)]
        far = lax.ppermute(array[-blocks:], "context", ahead)
        return jnp.concatenate([far, array], axis=0)

    blocks = halo // rows
    message = exchange(pack(readout, segments, loss_mask, labels, queries, keys, values))
    later, message = lax.optimization_barrier((pack_later(grad_out, values), message))
    later = exchange(later)
    own, other = split(message)
    lines = message[:, rows + rows // 2 :]
    flag = jnp.stack([lines[:, MASK], lines[:, LABEL]]).astype(f32)
    lines, own, other = from_before(lines), from_before(own), from_before(other)
    seg = lines[:, SEGMENT].astype(jnp.int32)
    if many:
        place_of = jnp.arange(blocks + heads, dtype=jnp.int32)[:, None]
        seg = jnp.where((index < heads) & (place_of < blocks), -1, seg)
    where = jnp.reshape(index, (1,)).astype(jnp.int32)
    total, reward, starts = attention_forward(halo, where, message, own, other, seg, lines)

    for step in (1, 2, 4, 8):
        reward = reward + lax.ppermute(reward, "context", [(i, i ^ step) for i in range(devices)])

    later, reward = lax.optimization_barrier((later, reward))
    own_value, other_value = split(later)
    query_grad, keep, send = attention_backward(
        halo, where, starts, message, own, other, later, from_before(own_value),
        from_before(other_value), readout, reward, flag, total,
    )
    total = keep.astype(f32) + swap(send).astype(f32)
    if many:
        behind = [(i + heads, i) for i in range(devices - heads)]
        back = lax.ppermute(total[:blocks].astype(bf16), "context", behind)
        total = total[blocks:]
        total = total + jnp.pad(
            back.astype(f32), ((heads - blocks, 0), (0, 0), (0, 0))
        )
    home = exchange(jnp.concatenate([query_grad, total.astype(bf16)], axis=1))
    return unpack(home, queries, keys, values)


def solution(mesh):
    sharded = P(("groups", "context"))
    return jax.shard_map(
        local,
        mesh=mesh,
        in_specs=(sharded,) * 4 + (P(),) + (sharded,) * 3,
        out_specs=(sharded,) * 3,
        check_vma=False,
    )
```

```python
import functools
import math

import jax
import jax.numpy as jnp
from jax import lax
from jax.experimental import pallas as pl
from jax.experimental.pallas import tpu as pltpu
from jax.sharding import PartitionSpec as P

WINDOW = 1024
SCALE = 168.0 ** (-0.5)
LOG2E = math.log2(math.e)
NEGATIVE = -1e30
BLOCK = 256
AUX = 8
SEGMENT, MASK, LABEL = 3, 4, 5
QUERIES = 2 * BLOCK
REACH = (WINDOW + QUERIES) // BLOCK
VMEM = pl.BlockSpec(memory_space=pltpu.VMEM)
ANY = pl.BlockSpec(memory_space=pl.ANY)
SMEM = pl.BlockSpec(memory_space=pltpu.SMEM)
NT = (((1,), (1,)), ((), ()))
NN = (((1,), (0,)), ((), ()))


def dot(a, b, dims):
    return lax.dot_general(a, b, dims, preferred_element_type=jnp.float32)


def starts_of(seg_all):
    return [jnp.sum(jnp.where(seg_all < s, 1, 0)) for s in range(4)]


def begin_of(starts, token):
    begin = token - (WINDOW - 1)
    for start in starts:
        begin = jnp.maximum(begin, jnp.where(start <= token, start, 0))
    return begin


def tokens_of(tokens, halo):
    shape = (tokens // QUERIES, QUERIES)
    row = lax.broadcasted_iota(jnp.int32, shape, 0)
    return halo + row * QUERIES + lax.broadcasted_iota(jnp.int32, shape, 1)


def rows_of(block):
    return pl.ds(pl.multiple_of(block * BLOCK, BLOCK), BLOCK)


def by_reach(count, body):
    for n in range(2, REACH + 1):
        pl.when(count == n)(functools.partial(body, n))


def late(j, n):
    if j == n - 1:
        return slice(BLOCK, QUERIES)
    return slice(0, BLOCK if j == 0 and n == REACH else QUERIES)


def valid_of(key_iota, causal, bound, j, n):
    span = late(j, n)
    valid = key_iota[:, span] >= bound[:, span] - j * BLOCK
    if j == n - 1:
        return valid & causal[:, :BLOCK]
    return valid & causal if j == n - 2 else valid


def fold(parts, combine, reduce):
    if reduce is not None:
        parts = [reduce(p.reshape(p.shape[0] // 8, 8, p.shape[1]), axis=0) for p in parts]
    whole = functools.reduce(combine, [p for p in parts if p.shape[1] == QUERIES])
    early, later = whole[:, :BLOCK], combine(whole[:, BLOCK:], parts[-1])
    if parts[0].shape[1] == BLOCK:
        early = combine(early, parts[0])
    return jnp.concatenate([early, later], axis=1)


def place(even, own_ref, other_ref, put):
    def both(first, second):
        for n in range(first.shape[0]):
            put(n, jnp.concatenate([first[n], second[n]], axis=0))

    pl.when(even)(lambda: both(own_ref, other_ref))
    pl.when(jnp.logical_not(even))(lambda: both(other_ref, own_ref))


def forward_kernel(
    halo, index_ref, message_ref, own_ref, other_ref, seg_ref, lines_ref,
    total_ref, reward_ref, starts_ref,
    key_s, side_s, bound_s,
):
    tokens = message_ref.shape[0] * 128
    shift = halo // BLOCK
    even = lax.rem(index_ref[0], 2) == 0
    low_bits = jnp.bfloat16
    for n in range(lines_ref.shape[0]):
        side_s[:, n * 128 : (n + 1) * 128] = lines_ref[n]

    def put(n, keys):
        key_s[n * 128 : (n + 1) * 128, :] = keys

    place(even, own_ref, other_ref, put)
    starts = starts_of(seg_ref[...])
    for n, start in enumerate(starts):
        starts_ref[n] = start
    bound_s[...] = begin_of(starts, tokens_of(tokens, halo))
    key_iota = lax.broadcasted_iota(jnp.int32, (BLOCK, QUERIES), 0)
    query_iota = lax.broadcasted_iota(jnp.int32, (BLOCK, QUERIES), 1)
    causal = key_iota <= query_iota

    def query_block(i, _):
        first = lax.div(begin_of(starts, halo + i * QUERIES), BLOCK)

        def body(n):
            query = message_ref[pl.ds(4 * i, 4), 0:128, :].reshape(QUERIES, 128)
            bound = bound_s[pl.ds(i, 1), :] - first * BLOCK
            scores = []
            for j in range(n):
                span = late(j, n)
                score = dot(key_s[rows_of(first + j), :], query[span], NT)
                scores.append(jnp.where(valid_of(key_iota, causal, bound, j, n), score, NEGATIVE))
            top = jnp.max(fold(scores, jnp.maximum, jnp.max), axis=0, keepdims=True)
            sums = []
            for j in range(n):
                prob = jnp.exp2((scores[j] - top[:, late(j, n)]) * (SCALE * LOG2E))
                sums.append(dot(side_s[:, rows_of(first + j)], prob.astype(low_bits), NN))
            sums = fold(sums, jnp.add, None)
            reward = (sums[0:1] + sums[1:2]) / sums[2:3]
            total_ref[pl.ds(i, 1), :] = top * (SCALE * LOG2E) + jnp.log2(sums[2:3])
            for part in range(4):
                reward_ref[pl.ds(4 * i + part, 1), :] = reward[:, part * 128 : (part + 1) * 128]

        by_reach(2 * i + 2 + shift - first, body)
        return 0

    lax.fori_loop(0, tokens // QUERIES, query_block, 0)


def backward_kernel(
    halo, index_ref, starts_ref, message_ref, own_ref, other_ref, later_ref, own_value_ref,
    other_value_ref, readout_ref, reward_ref, flag_ref, total_ref,
    query_ref, keep_ref, send_ref,
    key_s, turned_s, value_s, grad_s, bound_s, key_grad_s, value_grad_s,
):
    heads, tokens = message_ref.shape[0], message_ref.shape[0] * 128
    shift = halo // BLOCK
    index = index_ref[0]
    head = lax.rem(index, heads)
    even = lax.rem(index, 2) == 0

    def put_key(n, keys):
        key_s[n * 128 : (n + 1) * 128, :] = keys
        turned_s[:, n * 128 : (n + 1) * 128] = keys.T

    def put_value(n, values):
        value_s[n * 128 : (n + 1) * 128, :] = values

    place(even, own_ref, other_ref, put_key)
    place(even, own_value_ref, other_value_ref, put_value)

    live = flag_ref[0]
    probe = live * (jax.nn.sigmoid(reward_ref[...]) - flag_ref[1])
    live_t, probe_t = live.T, probe.T
    weights = readout_ref[pl.ds(head, 1), :]
    for s in range(heads):
        grad = live_t[:, s : s + 1] * later_ref[s, 0:128, :].astype(jnp.float32)
        grad_s[s] = (grad + probe_t[:, s : s + 1] * weights).astype(jnp.bfloat16)

    starts = [starts_ref[n] for n in range(4)]
    bound_s[...] = begin_of(starts, tokens_of(tokens, halo))
    key_iota = lax.broadcasted_iota(jnp.int32, (BLOCK, QUERIES), 0)
    query_iota = lax.broadcasted_iota(jnp.int32, (BLOCK, QUERIES), 1)
    causal = key_iota <= query_iota
    if halo:
        key_grad_s[:halo, :] = jnp.zeros((halo, 128), jnp.float32)
        value_grad_s[:halo, :] = jnp.zeros((halo, 128), jnp.float32)

    def query_block(i, _):
        first = lax.div(begin_of(starts, halo + i * QUERIES), BLOCK)

        def body(n):
            grad = grad_s[pl.ds(4 * i, 4)].reshape(QUERIES, 128)
            query = message_ref[pl.ds(4 * i, 4), 0:128, :].reshape(QUERIES, 128)
            bound = bound_s[pl.ds(i, 1), :] - first * BLOCK
            total = total_ref[pl.ds(i, 1), :]
            probs, grad_probs, deltas = [], [], []

            def dots(j):
                rows, span = rows_of(first + j), late(j, n)
                return dot(key_s[rows, :], query[span], NT), dot(value_s[rows, :], grad[span], NT)

            ahead = dots(0)
            for j in range(n):
                rows, span = rows_of(first + j), late(j, n)
                score, grad_prob = ahead
                if j < n - 1:
                    ahead = dots(j + 1)
                score = score * (SCALE * LOG2E) - total[:, span]
                valid = valid_of(key_iota, causal, bound, j, n)
                prob = jnp.exp2(jnp.where(valid, score, NEGATIVE))
                deltas.append(prob * grad_prob)
                value_grad = dot(prob.astype(jnp.bfloat16), grad[span], NN)
                if j >= n - 2:
                    value_grad_s[rows, :] = value_grad
                else:
                    value_grad_s[rows, :] += value_grad
                probs.append(prob)
                grad_probs.append(grad_prob)
            delta = jnp.sum(fold(deltas, jnp.add, jnp.sum), axis=0, keepdims=True)
            query_grads = []
            for j in range(n):
                rows, span = rows_of(first + j), late(j, n)
                grad_score = (probs[j] * (grad_probs[j] - delta[:, span])).astype(jnp.bfloat16)
                key_grad = dot(grad_score, query[span], NN)
                if j >= n - 2:
                    key_grad_s[rows, :] = key_grad
                else:
                    key_grad_s[rows, :] += key_grad
                query_grads.append(dot(turned_s[:, rows], grad_score, NN))
            query_grad = (fold(query_grads, jnp.add, None) * SCALE).T.astype(jnp.bfloat16)
            query_ref[pl.ds(4 * i, 4)] = query_grad.reshape(4, 128, 128)

        by_reach(2 * i + 2 + shift - first, body)
        return 0

    lax.fori_loop(0, tokens // QUERIES, query_block, 0)
    shape = keep_ref.shape

    @pl.when(even)
    def _():
        keep_ref[...] = (key_grad_s[...] * SCALE).astype(jnp.bfloat16).reshape(shape)
        send_ref[...] = value_grad_s[...].astype(jnp.bfloat16).reshape(shape)

    @pl.when(jnp.logical_not(even))
    def _():
        keep_ref[...] = value_grad_s[...].astype(jnp.bfloat16).reshape(shape)
        send_ref[...] = (key_grad_s[...] * SCALE).astype(jnp.bfloat16).reshape(shape)


def attention_forward(halo, where, message, own, other, seg, lines):
    heads, depth = message.shape[0], message.shape[2]
    key_tokens = own.shape[0] * 128
    count = message.shape[0] * 128 // QUERIES
    return pl.pallas_call(
        functools.partial(forward_kernel, halo),
        out_shape=(
            jax.ShapeDtypeStruct((count, QUERIES), jnp.float32),
            jax.ShapeDtypeStruct((heads, 128), jnp.float32),
            jax.ShapeDtypeStruct((4,), jnp.int32),
        ),
        in_specs=[SMEM] + [VMEM] * 5,
        out_specs=(VMEM, VMEM, SMEM),
        scratch_shapes=[
            pltpu.VMEM((key_tokens, depth), jnp.bfloat16),
            pltpu.VMEM((8, key_tokens), jnp.bfloat16),
            pltpu.VMEM((count, QUERIES), jnp.int32),
        ],
        compiler_params=pltpu.CompilerParams(vmem_limit_bytes=24 << 20),
        cost_estimate=pl.CostEstimate(
            flops=4 * BLOCK * QUERIES * depth * count * REACH,
            bytes_accessed=16 << 20,
            transcendentals=BLOCK * QUERIES * count * REACH,
        ),
        name="attention_forward",
    )(where, message, own, other, seg, lines)


def attention_backward(
    halo, where, starts, message, own, other, later, own_value, other_value, readout, reward, flag, total
):
    heads, depth = message.shape[0], message.shape[2]
    key_tokens = own.shape[0] * 128
    count = message.shape[0] * 128 // QUERIES
    return pl.pallas_call(
        functools.partial(backward_kernel, halo),
        out_shape=(
            jax.ShapeDtypeStruct((heads, 128, depth), jnp.bfloat16),
            jax.ShapeDtypeStruct((own.shape[0], 128, depth), jnp.bfloat16),
            jax.ShapeDtypeStruct((own.shape[0], 128, depth), jnp.bfloat16),
        ),
        in_specs=[SMEM, SMEM] + [VMEM] * 10,
        out_specs=(VMEM, VMEM, VMEM),
        scratch_shapes=[
            pltpu.VMEM((key_tokens, depth), jnp.bfloat16),
            pltpu.VMEM((depth, key_tokens), jnp.bfloat16),
            pltpu.VMEM((key_tokens, depth), jnp.bfloat16),
            pltpu.VMEM((heads, 128, depth), jnp.bfloat16),
            pltpu.VMEM((count, QUERIES), jnp.int32),
            pltpu.VMEM((key_tokens, depth), jnp.float32),
            pltpu.VMEM((key_tokens, depth), jnp.float32),
        ],
        compiler_params=pltpu.CompilerParams(vmem_limit_bytes=24 << 20),
        cost_estimate=pl.CostEstimate(
            flops=10 * BLOCK * QUERIES * depth * count * REACH,
            bytes_accessed=16 << 20,
            transcendentals=0,
        ),
        name="attention_backward",
    )(
        where, starts, message, own, other, later, own_value, other_value,
        readout, reward, flag, total,
    )


def halves_into(target, start, heads):
    half = heads.shape[1] // 2
    for h in range(2 * heads.shape[0]):
        part = h % 2 * half
        target[h, start : start + half, :] = heads[h // 2, part : part + half]


def pack_kernel(
    readout_ref, segments_ref, mask_ref, labels_ref, queries_ref, keys_ref, values_ref,
    message_ref, readout_s, segments_s, mask_s, labels_s, query_s, key_s, value_s, message_s,
    in_sems, out_sems,
):
    rows, kv_heads = keys_ref.shape[:2]
    pairs = [
        (queries_ref, query_s), (values_ref, value_s), (keys_ref, key_s), (readout_ref, readout_s),
        (segments_ref, segments_s), (mask_ref, mask_s), (labels_ref, labels_s),
    ]
    copies = [
        pltpu.make_async_copy(source, target, in_sems.at[n])
        for n, (source, target) in enumerate(pairs)
    ]
    for copy in copies:
        copy.start()

    def send(n, first, last):
        part = (slice(None), slice(first, last))
        return pltpu.make_async_copy(message_s.at[part], message_ref.at[part], out_sems.at[n])

    copies[0].wait()
    message_s[:, :rows, :] = jnp.swapaxes(query_s[...], 0, 1)
    first = send(0, 0, rows)
    first.start()
    copies[2].wait()
    halves_into(message_s, rows, jnp.swapaxes(key_s[...], 0, 1))
    second = send(1, rows, rows + rows // 2)
    second.start()
    for copy in copies[3:]:
        copy.wait()
    readout = readout_s[...]
    high = readout.astype(jnp.bfloat16).astype(jnp.float32)
    middle = (readout - high).astype(jnp.bfloat16).astype(jnp.float32)
    rest = readout - high - middle
    spare = jnp.zeros((2, readout.shape[1]), jnp.float32)
    line = lax.broadcasted_iota(jnp.int32, (AUX, rows), 0)
    flags = jnp.ones((AUX, rows), jnp.float32)
    for n, source in ((SEGMENT, segments_s), (MASK, mask_s), (LABEL, labels_s)):
        flags = jnp.where(line == n, source[...].reshape(1, rows).astype(jnp.float32), flags)
    copies[1].wait()
    values = jnp.swapaxes(value_s[...], 0, 1)
    for c in range(kv_heads):
        parts = [p[h : h + 1] for h in (2 * c, 2 * c + 1) for p in (high, middle, rest)]
        weights = jnp.concatenate(parts + [spare], axis=0).astype(jnp.bfloat16)
        product = dot(weights, values[c], NT)
        for h in range(2):
            worth = product[3 * h : 3 * h + 1] + product[3 * h + 1 : 3 * h + 2]
            worth = worth + product[3 * h + 2 : 3 * h + 3]
            worth_high = worth.astype(jnp.bfloat16).astype(jnp.float32)
            lines = jnp.where(line == 0, worth_high, jnp.where(line == 1, worth - worth_high, flags))
            message_s[2 * c + h, rows + rows // 2 :, :] = lines.astype(jnp.bfloat16)
    third = send(2, rows + rows // 2, rows + rows // 2 + AUX)
    third.start()
    first.wait()
    second.wait()
    third.wait()


def pack(readout, segments, loss_mask, labels, queries, keys, values):
    rows, heads, depth = queries.shape
    shape = (heads, rows + rows // 2 + AUX, depth)
    return pl.pallas_call(
        pack_kernel,
        out_shape=jax.ShapeDtypeStruct(shape, jnp.bfloat16),
        in_specs=[ANY] * 7,
        out_specs=ANY,
        scratch_shapes=[
            pltpu.VMEM(readout.shape, jnp.float32),
            pltpu.VMEM(segments.shape, jnp.int32),
            pltpu.VMEM(segments.shape, jnp.int32),
            pltpu.VMEM(segments.shape, jnp.int32),
            pltpu.VMEM(queries.shape, jnp.bfloat16),
            pltpu.VMEM(keys.shape, jnp.bfloat16),
            pltpu.VMEM(values.shape, jnp.bfloat16),
            pltpu.VMEM(shape, jnp.bfloat16),
            pltpu.SemaphoreType.DMA((7,)),
            pltpu.SemaphoreType.DMA((3,)),
        ],
        compiler_params=pltpu.CompilerParams(vmem_limit_bytes=60 << 20),
        name="pack",
    )(readout, segments, loss_mask, labels, queries, keys, values)


def pack_later_kernel(grad_ref, values_ref, message_ref):
    rows = grad_ref.shape[0]
    message_ref[:, :rows, :] = jnp.swapaxes(grad_ref[...], 0, 1)
    halves_into(message_ref, rows, jnp.swapaxes(values_ref[...], 0, 1))


def pack_later(grad_out, values):
    rows, heads, depth = grad_out.shape
    return pl.pallas_call(
        pack_later_kernel,
        out_shape=jax.ShapeDtypeStruct((heads, rows + rows // 2, depth), jnp.bfloat16),
        in_specs=[VMEM] * 2,
        out_specs=VMEM,
        compiler_params=pltpu.CompilerParams(vmem_limit_bytes=16 << 20),
        cost_estimate=pl.CostEstimate(flops=0, bytes_accessed=3 << 20, transcendentals=0),
        name="pack_later",
    )(grad_out, values)


def unpack_kernel(home_ref, query_ref, key_ref, value_ref):
    rows = query_ref.shape[0]
    heads = home_ref.shape[0]
    query_ref[...] = jnp.swapaxes(home_ref[:, :rows, :], 0, 1)
    for parity, target in enumerate((key_ref, value_ref)):
        parts = [home_ref[h : h + 1, rows:, :] for h in range(parity, heads, 2)]
        target[...] = jnp.swapaxes(jnp.concatenate(parts, axis=0), 0, 1)


def unpack(home, queries, keys, values):
    return pl.pallas_call(
        unpack_kernel,
        out_shape=tuple(jax.ShapeDtypeStruct(a.shape, a.dtype) for a in (queries, keys, values)),
        in_specs=[VMEM],
        out_specs=(VMEM,) * 3,
        compiler_params=pltpu.CompilerParams(vmem_limit_bytes=24 << 20),
        name="unpack",
    )(home)


def local(queries, keys, values, grad_out, readout, segments, loss_mask, labels):
    rows, heads, depth = queries.shape
    devices = lax.axis_size("context")
    index = lax.axis_index("context")
    clusters = [list(range(s, s + heads)) for s in range(0, devices, heads)]
    many = len(clusters) > 1
    halo = WINDOW if many else 0
    pairs = [(i, i ^ 1) for i in range(devices)]
    bf16, f32 = jnp.bfloat16, jnp.float32

    def exchange(array):
        return lax.all_to_all(
            array, "context", 0, 0, tiled=True, axis_index_groups=clusters if many else None
        )

    def swap(array):
        return lax.ppermute(array, "context", pairs)

    def split(array):
        own = array[:, rows : rows + rows // 2]
        return own, swap(own)

    def from_before(array):
        if not many:
            return array
        ahead = [(i, i + heads) for i in range(devices - heads)]
        far = lax.ppermute(array[-blocks:], "context", ahead)
        return jnp.concatenate([far, array], axis=0)

    blocks = halo // rows
    message = exchange(pack(readout, segments, loss_mask, labels, queries, keys, values))
    later, message = lax.optimization_barrier((pack_later(grad_out, values), message))
    later = exchange(later)
    own, other = split(message)
    lines = message[:, rows + rows // 2 :]
    flag = jnp.stack([lines[:, MASK], lines[:, LABEL]]).astype(f32)
    lines, own, other = from_before(lines), from_before(own), from_before(other)
    seg = lines[:, SEGMENT].astype(jnp.int32)
    if many:
        place_of = jnp.arange(blocks + heads, dtype=jnp.int32)[:, None]
        seg = jnp.where((index < heads) & (place_of < blocks), -1, seg)
    where = jnp.reshape(index, (1,)).astype(jnp.int32)
    total, reward, starts = attention_forward(halo, where, message, own, other, seg, lines)

    for step in (2, 1, 4, 8):
        reward = reward + lax.ppermute(reward, "context", [(i, i ^ step) for i in range(devices)])

    later, reward = lax.optimization_barrier((later, reward))
    own_value, other_value = split(later)
    query_grad, keep, send = attention_backward(
        halo, where, starts, message, own, other, later, from_before(own_value),
        from_before(other_value), readout, reward, flag, total,
    )
    total = keep.astype(f32) + swap(send).astype(f32)
    if many:
        behind = [(i + heads, i) for i in range(devices - heads)]
        back = lax.ppermute(total[:blocks].astype(bf16), "context", behind)
        total = total[blocks:]
        total = total + jnp.pad(
            back.astype(f32), ((heads - blocks, 0), (0, 0), (0, 0))
        )
    home = exchange(jnp.concatenate([query_grad, total.astype(bf16)], axis=1))
    return unpack(home, queries, keys, values)


def solution(mesh):
    sharded = P(("groups", "context"))
    return jax.shard_map(
        local,
        mesh=mesh,
        in_specs=(sharded,) * 4 + (P(),) + (sharded,) * 3,
        out_specs=(sharded,) * 3,
        check_vma=False,
    )
```
